32 devices in a mesh: grp: 2 (over y), row: 8 (over z, x), col: 2 (over core).
Axes of the slice: x: 2, y: 2, z: 4, core: 2. Of those that a mesh axis runs over, the one named last changes fastest.
Arguments:
- features: bfloat16 [128, 128, 256], P(('grp', 'row'), 'col'), parts along dimension 0, may hold values from -6 to 6
- cotangent: bfloat16 [128, 128, 256], P(('grp', 'row'), 'col'), parts along dimension 0, may hold values from -6 to 6
- domain: int32 [128, 128], P(('grp', 'row'), 'col'), parts along dimension 0, may hold values 0 or 1
- qkv_weight: bfloat16 [256, 768], replicated, may hold values from -6 to 6
- proj_weight: bfloat16 [256, 256], replicated, may hold values from -0.375 to 0.375
- norm_gain: float32 [256], replicated, may hold values from 0.5 to 1.5
Outputs:
- updated: bfloat16 [128, 128, 256], P(('grp', 'row'), 'col'), parts along dimension 0
- grad_features: bfloat16 [128, 128, 256], P(('grp', 'row'), 'col'), parts along dimension 0
- grad_qkv: float32 [512, 768], P('grp'), parts along dimension 0
- grad_proj: float32 [512, 256], P('grp'), parts along dimension 0
- grad_gain: float32 [512], P('grp'), parts along dimension 0
The draws below stay inside these ranges and needn't reach their ends.
There are 2 independent parts, one for each index of `grp`. The reference program is written for one: setup_inputs(seed, part) draws one part's arguments, and reference() takes and returns one part's arrays. A program takes and returns all parts, laid end to end along the dimension named above; an argument that names none is the same for every part. Nothing has to cross between parts.
All inputs are finite; a program needn't handle non-finite values. No bound on the sum of `domain` on one device may be relied on, other than what follows from the above.
Results may differ from the reference program's by a relative error of at most 0.013.
Values may be sent and summed in bfloat16 or wider, within the bound.
No kernel may reach another device: no remote copies, remote signals or barrier semaphores. Data moves between devices by JAX's collectives and lax.ppermute only.
A program may use at most 64 MiB of HBM per device.

```python
import jax
import jax.numpy as jnp
from jax import lax

D = 256
HEADS = 8
WIN = 8
SHIFT = 4
HEIGHT = 64
WIDTH = 128


def draw_qkv_weight(key, part):
    return (jax.random.normal(key, (D, 3 * D), jnp.float32) * D ** (-0.5)).astype(jnp.bfloat16)


def touch_ends(drawn, key, low, high):
    longest = drawn.shape.index(max(drawn.shape))
    spots = []
    for shift in (0, 1):
        where = [jax.random.randint(jax.random.fold_in(key, axis), (), 0, length) for axis, length in enumerate(drawn.shape)]
        where[longest] = (where[longest] + shift) % drawn.shape[longest]
        spots.append(tuple(where))
    return drawn.at[spots[0]].set(low).at[spots[1]].set(high)


def levels(own_key, shape, shards, least, high):
    level, own = 1.0, jax.random.fold_in(own_key, 6)
    for axis_at, blocks in shards:
        heights = jnp.exp(jax.random.uniform(jax.random.fold_in(own, axis_at), (blocks,), jnp.float32, least / len(shards), high / len(shards)))
        level = level * jnp.repeat(heights, shape[axis_at] // blocks).reshape([-1 if axis == axis_at else 1 for axis in range(len(shape))])
    return level


def noise(stream_key, dims, width, reach, cuts=(), kind=jnp.bfloat16):
    factor_of = levels(stream_key, dims, cuts, -0.22, 0.18) if cuts else 1.0
    drawn = jax.random.normal(stream_key, dims, jnp.float32) * width * factor_of
    return jnp.minimum(jnp.maximum(drawn, -reach), reach).astype(kind)


def setup_inputs(seed: int = 0, part: int = 0) -> dict:
    splits = jax.random.split(jax.random.key(seed), 7)
    part_keys = jax.random.split(jax.random.fold_in(splits[6], part), 7)
    features = noise(part_keys[0], (HEIGHT, WIDTH, D), 1.0, 6.0, ((0, 8), (1, 2)))
    cotangent = noise(part_keys[1], (HEIGHT, WIDTH, D), 1.0, 6.0, ((0, 8), (1, 2)))
    domain = touch_ends((jax.random.randint(part_keys[2], (HEIGHT, WIDTH), 0, 4) < 3).astype(jnp.int32), jax.random.fold_in(part_keys[2], 1), 0, 1)
    qkv_weight = draw_qkv_weight(jax.random.fold_in(splits[6], 71), part)
    proj_weight = noise(splits[4], (D, D), D ** -0.5, 0.375)
    norm_gain = jnp.clip(1.0 + 0.1 * jax.random.normal(splits[5], (D,), jnp.float32), 0.5, 1.5)
    return dict(features=features, cotangent=cotangent, domain=domain, qkv_weight=qkv_weight, proj_weight=proj_weight, norm_gain=norm_gain)


NORM_EPSILON = 1e-05
MASKED_SCORE = -1e+30

def layer_norm(values, norm_gain):
    average = lax.optimization_barrier(jnp.mean(values, -1, keepdims=True))
    centred = values - average
    variance = lax.optimization_barrier(jnp.mean(centred * centred, -1, keepdims=True))
    return centred * lax.rsqrt(variance + NORM_EPSILON) * norm_gain

def region_of(cell_ids, extent):
    return (cell_ids >= extent - WIN).astype(jnp.int32) + (cell_ids >= extent - SHIFT).astype(jnp.int32)

def region_labels(row_start, tile_rows, total_rows, col_start, tile_cols, total_cols):
    row_ids = row_start + jnp.arange(tile_rows, dtype=jnp.int32)
    col_ids = col_start + jnp.arange(tile_cols, dtype=jnp.int32)
    return region_of(row_ids, total_rows)[:, None] * 3 + region_of(col_ids, total_cols)[None, :]

def contract_rows(left, right):
    return lax.dot_general(left, right, (((0,), (0,)), ((), ())), preferred_element_type=jnp.float32)

def contract_cols(left, right):
    return lax.dot_general(left, right, (((1,), (1,)), ((), ())), preferred_element_type=jnp.float32)

def window_core(projected, labels):
    tile_rows, tile_cols, triple = projected.shape
    channels = triple // 3
    windows = tile_cols // WIN
    head_dim = channels // HEADS
    grouped = projected.reshape(tile_rows, windows, WIN, triple).transpose(1, 0, 2, 3).reshape(windows, tile_rows * WIN, triple)
    grouped_labels = labels.reshape(tile_rows, windows, WIN).transpose(1, 0, 2).reshape(windows, tile_rows * WIN)
    query_part = grouped[:, :, :channels].reshape(windows, -1, HEADS, head_dim)
    key_part = grouped[:, :, channels:2 * channels].reshape(windows, -1, HEADS, head_dim)
    value_part = grouped[:, :, 2 * channels:].reshape(windows, -1, HEADS, head_dim)
    scores = jnp.einsum('wqhd,wkhd->whqk', query_part, key_part) * head_dim ** (-0.5)
    allowed = (grouped_labels[:, :, None] == grouped_labels[:, None, :])[:, None]
    scores = jnp.where(allowed, scores, MASKED_SCORE)
    peak = lax.stop_gradient(lax.optimization_barrier(jnp.max(scores, -1, keepdims=True)))
    weights = jnp.exp(scores - peak)
    probability = weights / lax.optimization_barrier(jnp.sum(weights, -1, keepdims=True))
    probability = lax.optimization_barrier(probability.astype(jnp.bfloat16)).astype(jnp.float32)
    context = jnp.einsum('whqk,wkhd->wqhd', probability, value_part)
    context = context.reshape(windows, tile_rows, WIN, channels).transpose(1, 0, 2, 3).reshape(tile_rows, tile_cols, channels)
    return context.astype(jnp.bfloat16)

def forward_block(shifted, labels, qkv_weight, proj_weight):
    tile_rows, tile_cols, channels = shifted.shape
    flat_rows = shifted.reshape(-1, channels)
    projected = jnp.dot(flat_rows, qkv_weight, preferred_element_type=jnp.float32).astype(jnp.bfloat16)
    projected = projected.reshape(tile_rows, tile_cols, 3 * channels)
    context = window_core(projected.astype(jnp.float32), labels)
    attended = jnp.dot(context.reshape(-1, channels), proj_weight, preferred_element_type=jnp.float32).astype(jnp.bfloat16)
    return (projected, context, attended.reshape(shifted.shape))

def backward_block(shifted, labels, projected, context, dattended, qkv_weight, proj_weight):
    channels = shifted.shape[-1]
    grad_rows = dattended.reshape(-1, channels)
    grad_proj = contract_rows(context.reshape(-1, channels), grad_rows)
    dcontext = contract_cols(grad_rows, proj_weight).astype(jnp.bfloat16).reshape(context.shape)

    def core_only(values):
        return window_core(values, labels)
    _, pullback = jax.vjp(core_only, projected.astype(jnp.float32))
    dprojected = pullback(dcontext)[0].astype(jnp.bfloat16).reshape(-1, 3 * channels)
    grad_qkv = contract_rows(shifted.reshape(-1, channels), dprojected)
    dshifted = contract_cols(dprojected, qkv_weight).astype(jnp.bfloat16).reshape(shifted.shape)
    return (grad_qkv, grad_proj, dshifted)

def norm_backward(values, norm_gain, dnormed):

    def apply_norm(inputs):
        return layer_norm(inputs, norm_gain)
    _, pullback = jax.vjp(apply_norm, values)
    upstream = dnormed.astype(jnp.float32)
    grad_values = pullback(upstream)[0]
    standard = layer_norm(values, jnp.ones_like(norm_gain))
    grad_gain = lax.optimization_barrier(jnp.sum((upstream * standard).reshape(-1, values.shape[-1]), 0))
    return (grad_values, grad_gain)

def reference(features, cotangent, domain, qkv_weight, proj_weight, norm_gain):
    total_rows, total_cols, channels = features.shape
    values = features.astype(jnp.float32)
    normed = layer_norm(values, norm_gain).astype(jnp.bfloat16)
    shifted = jnp.roll(normed, (-SHIFT, -SHIFT), (0, 1))
    labels = region_labels(0, total_rows, total_rows, 0, total_cols, total_cols)
    bands = shifted.reshape(total_rows // WIN, WIN, total_cols, channels)
    band_labels = labels.reshape(total_rows // WIN, WIN, total_cols)

    def forward_step(inputs):
        return forward_block(inputs[0], inputs[1], qkv_weight, proj_weight)[2]
    attended = lax.map(forward_step, (bands, band_labels)).reshape(total_rows, total_cols, channels)
    inside = domain.astype(jnp.float32)[..., None]
    updated = (values + inside * jnp.roll(attended, (SHIFT, SHIFT), (0, 1)).astype(jnp.float32)).astype(jnp.bfloat16)
    masked_grad = cotangent * domain.astype(jnp.bfloat16)[..., None]
    dattended = jnp.roll(masked_grad, (-SHIFT, -SHIFT), (0, 1)).reshape(bands.shape)

    def backward_step(totals, inputs):
        band, tags, grad_band = inputs
        projected, context, _ = forward_block(band, tags, qkv_weight, proj_weight)
        part_qkv, part_proj, dshifted = backward_block(band, tags, projected, context, grad_band, qkv_weight, proj_weight)
        return ((totals[0] + part_qkv, totals[1] + part_proj), dshifted)
    zeros_init = (jnp.zeros((channels, 3 * channels), jnp.float32), jnp.zeros((channels, channels), jnp.float32))
    (grad_qkv, grad_proj), dshifted = lax.scan(backward_step, zeros_init, (bands, band_labels, dattended))
    dnormed = jnp.roll(dshifted.reshape(total_rows, total_cols, channels), (SHIFT, SHIFT), (0, 1))
    grad_values, grad_gain = norm_backward(values, norm_gain, dnormed)
    grad_features = (cotangent.astype(jnp.float32) + grad_values).astype(jnp.bfloat16)
    return (updated, grad_features, grad_qkv, grad_proj, grad_gain)
```

```python
import jax
import jax.numpy as jnp
from jax import lax
from jax.experimental import pallas as pl
from jax.experimental.pallas import tpu as pltpu
from jax.sharding import PartitionSpec as P

HEADS = 8
WIN = 8
SHIFT = 4
NORM_EPSILON = 1e-05
MASKED_SCORE = -1e30
LOG2_E = 1.4426950408889634

BF16 = jnp.bfloat16
F32 = jnp.float32


def dot(left, right, left_dim, right_dim):
    return lax.dot_general(
        left, right, (((left_dim,), (right_dim,)), ((), ())), preferred_element_type=F32
    )


def assemble_shifted(buf, own, below, right, corner):
    cols = own.shape[1]
    buf[0:SHIFT, 0:cols, :] = own
    buf[SHIFT:WIN, 0:cols, :] = below[...].astype(F32)
    buf[0:SHIFT, cols : cols + WIN, :] = right[...].astype(F32)
    buf[SHIFT:WIN, cols : cols + WIN, :] = corner[...].astype(F32)


def domain_rows(domain, rows, channels):
    flags = domain[...].astype(F32).astype(BF16)
    row_ids = lax.broadcasted_iota(jnp.int32, (flags.shape[0], channels), 0)
    return [dot(flags, (row_ids == row).astype(F32).astype(BF16), 0, 0) for row in rows]


def block_kernel(
    feat, feat_below, feat_right, feat_corner,
    cot, cot_below, cot_right, cot_corner,
    domain, wqkv, wproj, gain,
    keep, send, ad_keep, ad_send,
    buf, shifted, projected, dattended, dcontext, context, dprojected, grads,
):
    tile_rows, cols, channels = feat.shape
    windows = cols // WIN
    cells = WIN * WIN
    half = channels // 2
    group_heads = HEADS // 2
    head_dim = channels // HEADS

    assemble_shifted(buf, feat[SHIFT:WIN].astype(F32), feat_below, feat_right, feat_corner)
    for w in range(windows):
        x = buf[:, SHIFT + WIN * w : SHIFT + WIN * (w + 1), :].reshape(cells, channels)
        centred = x - jnp.mean(x, -1, keepdims=True)
        variance = jnp.mean(centred * centred, -1, keepdims=True)
        normed = centred * lax.rsqrt(variance + NORM_EPSILON) * gain[...]
        shifted[cells * w : cells * (w + 1), :] = normed.astype(BF16)

    masks = domain_rows(domain, range(SHIFT, WIN), channels)
    own = jnp.stack([cot[SHIFT + i].astype(F32) * masks[i] for i in range(SHIFT)], 0)
    assemble_shifted(buf, own, cot_below, cot_right, cot_corner)
    for w in range(windows):
        x = buf[:, SHIFT + WIN * w : SHIFT + WIN * (w + 1), :].reshape(cells, channels)
        dattended[cells * w : cells * (w + 1), :] = x.astype(BF16)

    step = 128
    for m in range(0, cells * windows, step):
        projected[m : m + step, :] = dot(shifted[m : m + step, :], wqkv[...], 1, 0).astype(BF16)
        dcontext[m : m + step, :] = dot(dattended[m : m + step, :], wproj[...], 1, 1).astype(BF16)

    last_row = lax.axis_index("row") == lax.axis_size("row") - 1
    last_col = lax.axis_index("col") == lax.axis_size("col") - 1
    wide = group_heads * cells
    key_id = lax.broadcasted_iota(jnp.int32, (cells, wide), 0)
    query_id = lax.broadcasted_iota(jnp.int32, (cells, wide), 1)
    row_apart = ((key_id ^ query_id) & (WIN * SHIFT)) != 0
    col_apart = ((key_id ^ query_id) & SHIFT) != 0
    lane = lax.broadcasted_iota(jnp.int32, (cells, half), 1)
    in_head = [lane // head_dim == h for h in range(group_heads)]
    scale = head_dim ** (-0.5)

    def spread(values):
        zero = jnp.zeros_like(values)
        return jnp.concatenate([jnp.where(m, values, zero) for m in in_head], 0)

    def gather(full):
        parts = [full[cells * h : cells * (h + 1)] for h in range(group_heads)]
        out = parts[-1]
        for h in range(group_heads - 2, -1, -1):
            out = jnp.where(in_head[h], parts[h], out)
        return out

    def one_window(base, excluded):
        for g in range(2):
            at = half * g
            rows = pl.ds(base, cells)
            query = projected[rows, at : at + half]
            key = projected[rows, channels + at : channels + at + half]
            value = projected[rows, 2 * channels + at : 2 * channels + at + half]
            dctx = dcontext[rows, at : at + half]
            query_x = spread(query)
            dctx_x = spread(dctx)
            scores = dot(key, query_x, 1, 1)
            scores = jnp.where(excluded, MASKED_SCORE, scores)
            peak = jnp.max(scores, 0, keepdims=True)
            weights = jnp.exp2((scores - peak) * (scale * LOG2_E))
            probability = weights * (1.0 / jnp.sum(weights, 0, keepdims=True))
            prob16 = probability.astype(BF16)
            context[rows, at : at + half] = gather(dot(prob16, value, 0, 0)).astype(BF16)
            dprob = dot(value, dctx_x, 1, 1).astype(BF16).astype(F32)
            mean = jnp.sum(probability * dprob, 0, keepdims=True)
            dscore = (probability * (dprob - mean) * scale).astype(BF16)
            dprojected[rows, at : at + half] = gather(dot(dscore, key, 0, 0)).astype(BF16)
            dprojected[rows, channels + at : channels + at + half] = dot(
                dscore, query_x, 1, 0
            ).astype(BF16)
            dprojected[rows, 2 * channels + at : 2 * channels + at + half] = dot(
                prob16, dctx_x, 1, 0
            ).astype(BF16)

    row_excluded = jnp.logical_and(row_apart, last_row)
    for w in range(windows):
        excluded = row_excluded
        if w == windows - 1:
            excluded = jnp.logical_or(excluded, jnp.logical_and(col_apart, last_col))
        one_window(cells * w, excluded)

    for b in range(3):
        grads[channels * b : channels * (b + 1), :] = dot(
            shifted[...], dprojected[:, channels * b : channels * (b + 1)], 0, 0
        ).astype(BF16)
    grads[3 * channels : 4 * channels, :] = dot(context[...], dattended[...], 0, 0).astype(BF16)
    mine = lax.axis_index("col")
    keep[...] = grads[pl.ds(pl.multiple_of(mine * 2 * channels, 2 * channels), 2 * channels), :]
    send[...] = grads[
        pl.ds(pl.multiple_of((1 - mine) * 2 * channels, 2 * channels), 2 * channels), :
    ]

    def leave(slot):
        ad_keep[slot] = buf[0:SHIFT, 0:cols, :].astype(BF16)
        ad_send[slot] = buf[SHIFT:WIN, 0:cols, :].astype(BF16)

    for w in range(windows):
        rows = slice(cells * w, cells * (w + 1))
        buf[:, WIN * w : WIN * (w + 1), :] = dot(context[rows, :], wproj[...], 1, 0).reshape(
            WIN, WIN, channels
        )
    leave(0)
    for w in range(windows):
        rows = slice(cells * w, cells * (w + 1))
        buf[:, WIN * w : WIN * (w + 1), :] = dot(dprojected[rows, :], wqkv[...], 1, 1).reshape(
            WIN, WIN, channels
        )
    leave(1)


def finish_kernel(feat, cot, domain, gain, ad_keep, ad_rows, ad_cols, updated, grad_features, buf):
    tile_rows, cols, channels = feat.shape
    masks = domain_rows(domain, range(WIN), channels)

    def unshifted(slot):
        buf[:, 0:WIN, :] = ad_cols[slot].astype(F32)
        buf[0:SHIFT, WIN : WIN + cols, :] = ad_rows[slot].astype(F32)
        buf[SHIFT:WIN, WIN : WIN + cols, :] = ad_keep[slot].astype(F32)

    unshifted(0)
    for i in range(WIN):
        back = buf[i, SHIFT : SHIFT + cols, :]
        updated[i] = (feat[i].astype(F32) + masks[i] * back).astype(BF16)
    unshifted(1)
    for i in range(WIN):
        upstream = buf[i, SHIFT : SHIFT + cols, :] * gain[...]
        x = feat[i].astype(F32)
        centred = x - jnp.mean(x, -1, keepdims=True)
        variance = jnp.mean(centred * centred, -1, keepdims=True)
        inverse = lax.rsqrt(variance + NORM_EPSILON)
        standard = centred * inverse
        along = jnp.mean(upstream * standard, -1, keepdims=True)
        flat = jnp.mean(upstream, -1, keepdims=True)
        grad = inverse * (upstream - flat - standard * along)
        grad_features[i] = (cot[i].astype(F32) + grad).astype(BF16)


def sums_kernel(own, row_peer, col_peer, wqkv, gain, grad_qkv, grad_proj, grad_gain, blocks):
    channels = own.shape[0]
    mine_col = lax.axis_index("col")
    mine_row = lax.axis_index("row") % 2
    blocks[2 * mine_col + mine_row] = own[...].astype(F32)
    blocks[2 * mine_col + 1 - mine_row] = row_peer[...].astype(F32)
    other = 2 * (1 - mine_col)
    blocks[other] = col_peer[0:channels, :].astype(F32)
    blocks[other + 1] = col_peer[channels:, :].astype(F32)
    total = jnp.zeros((8, channels), F32)
    ones = jnp.ones((8, channels), BF16)
    for b in range(3):
        part = blocks[b]
        grad_qkv[:, channels * b : channels * (b + 1)] = part
        product = part * wqkv[:, channels * b : channels * (b + 1)].astype(F32)
        high = product.astype(BF16)
        low = (product - high.astype(F32)).astype(BF16)
        total = total + dot(ones, high, 1, 1) + dot(ones, low, 1, 1)
    grad_proj[...] = blocks[3]
    grad_gain[...] = total[0:1, :] / gain[...]


def run(kernel, out_shapes, scratch, *operands):
    return pl.pallas_call(
        kernel,
        out_shape=out_shapes,
        scratch_shapes=scratch,
        compiler_params=pltpu.CompilerParams(vmem_limit_bytes=48 << 20),
    )(*operands)


def ahead(array, axes):
    sizes = [lax.axis_size(a) for a in axes]
    if len(axes) == 1:
        pairs = [(i, (i - 1) % sizes[0]) for i in range(sizes[0])]
    else:
        rows, cols = sizes
        pairs = [
            (r * cols + c, (r - 1) % rows * cols + (c - 1) % cols)
            for r in range(rows)
            for c in range(cols)
        ]
    return lax.ppermute(array, axes if len(axes) > 1 else axes[0], pairs)


def behind(array, axis):
    peers = lax.axis_size(axis)
    return lax.ppermute(array, axis, [(i, (i + 1) % peers) for i in range(peers)])


def swap(array, axis, bit):
    return lax.ppermute(array, axis, [(i, i ^ bit) for i in range(lax.axis_size(axis))])


def add16(left, right):
    return (left.astype(F32) + right.astype(F32)).astype(BF16)


def on_device(features, cotangent, domain, qkv_weight, proj_weight, norm_gain):
    tile_rows, cols, channels = features.shape
    gain = norm_gain.reshape(1, channels)
    tokens = tile_rows * cols

    feat_below = ahead(features[:SHIFT], ("row",))
    feat_right = ahead(features[SHIFT:, :WIN], ("col",))
    feat_corner = ahead(features[:SHIFT, :WIN], ("row", "col"))
    flags = domain.astype(BF16)[..., None]
    cot_below = ahead(cotangent[:SHIFT] * flags[:SHIFT], ("row",))
    cot_right = ahead(cotangent[SHIFT:, :WIN] * flags[SHIFT:, :WIN], ("col",))
    cot_corner = ahead(cotangent[:SHIFT, :WIN] * flags[:SHIFT, :WIN], ("row", "col"))

    def shape(dims, dtype):
        return jax.ShapeDtypeStruct(dims, dtype)

    keep, send, ad_keep, ad_send = run(
        block_kernel,
        (
            shape((2 * channels, channels), BF16),
            shape((2 * channels, channels), BF16),
            shape((2, SHIFT, cols, channels), BF16),
            shape((2, SHIFT, cols, channels), BF16),
        ),
        [
            pltpu.VMEM((WIN, cols + WIN, channels), F32),
            pltpu.VMEM((tokens, channels), BF16),
            pltpu.VMEM((tokens, 3 * channels), BF16),
            pltpu.VMEM((tokens, channels), BF16),
            pltpu.VMEM((tokens, channels), BF16),
            pltpu.VMEM((tokens, channels), BF16),
            pltpu.VMEM((tokens, 3 * channels), BF16),
            pltpu.VMEM((4 * channels, channels), BF16),
        ],
        features, feat_below, feat_right, feat_corner,
        cotangent, cot_below, cot_right, cot_corner,
        domain, qkv_weight, proj_weight, gain,
    )

    summed = add16(keep, swap(send, "col", 1))
    mine_row = lax.axis_index("row") % 2
    mine = lax.dynamic_slice_in_dim(summed, mine_row * channels, channels, 0)
    other = lax.dynamic_slice_in_dim(summed, (1 - mine_row) * channels, channels, 0)
    own = add16(mine, swap(other, "row", 1))
    bit = 2
    while bit < lax.axis_size("row"):
        own = add16(own, swap(own, "row", bit))
        bit *= 2
    row_peer = swap(own, "row", 1)
    pair = jnp.where(
        mine_row == 0,
        jnp.concatenate([own, row_peer], 0),
        jnp.concatenate([row_peer, own], 0),
    )
    col_peer = swap(pair, "col", 1)
    grad_qkv, grad_proj, grad_gain = run(
        sums_kernel,
        (
            shape((channels, 3 * channels), F32),
            shape((channels, channels), F32),
            shape((1, channels), F32),
        ),
        [pltpu.VMEM((4, channels, channels), F32)],
        own, row_peer, col_peer, qkv_weight, gain,
    )

    ad_rows = behind(ad_send, "row")
    edge = jnp.concatenate([ad_rows[:, :, cols - WIN :], ad_keep[:, :, cols - WIN :]], 1)
    ad_cols = behind(edge, "col")
    updated, grad_features = run(
        finish_kernel,
        (shape(features.shape, BF16), shape(features.shape, BF16)),
        [pltpu.VMEM((WIN, cols + WIN, channels), F32)],
        features, cotangent, domain, gain, ad_keep, ad_rows, ad_cols,
    )
    return updated, grad_features, grad_qkv, grad_proj, grad_gain.reshape(channels)


def solution(mesh):
    return jax.shard_map(
        on_device,
        mesh=mesh,
        in_specs=(
            P(("grp", "row"), "col", None),
            P(("grp", "row"), "col", None),
            P(("grp", "row"), "col"),
            P(),
            P(),
            P(),
        ),
        out_specs=(
            P(("grp", "row"), "col", None),
            P(("grp", "row"), "col", None),
            P("grp", None),
            P("grp", None),
            P("grp"),
        ),
        check_vma=False,
    )
```

```python
import jax
import jax.numpy as jnp
from jax import lax
from jax.experimental import pallas as pl
from jax.experimental.pallas import tpu as pltpu
from jax.sharding import PartitionSpec as P

HEADS = 8
WIN = 8
SHIFT = 4
NORM_EPSILON = 1e-05
MASKED_SCORE = -1e30
LOG2_E = 1.4426950408889634

BF16 = jnp.bfloat16
F32 = jnp.float32


def dot(left, right, left_dim, right_dim):
    return lax.dot_general(
        left, right, (((left_dim,), (right_dim,)), ((), ())), preferred_element_type=F32
    )


def assemble_shifted(buf, own, below, right, corner):
    cols = own.shape[1]
    buf[0:SHIFT, 0:cols, :] = own
    buf[SHIFT:WIN, 0:cols, :] = below[...].astype(F32)
    buf[0:SHIFT, cols : cols + WIN, :] = right[...].astype(F32)
    buf[SHIFT:WIN, cols : cols + WIN, :] = corner[...].astype(F32)


def domain_rows(domain, rows, channels):
    flags = domain[...].astype(F32).astype(BF16)
    row_ids = lax.broadcasted_iota(jnp.int32, (flags.shape[0], channels), 0)
    return [dot(flags, (row_ids == row).astype(F32).astype(BF16), 0, 0) for row in rows]


def pack_kernel(
    feat, cot, domain_hbm, wqkv_hbm, wproj_hbm, gain_hbm,
    rows_out, right_out, corner_out, held, domain, wqkv, wproj, gain,
    sems,
):
    channels = feat.shape[-1]
    copies = [
        pltpu.make_async_copy(source, target, sems.at[i])
        for i, (source, target) in enumerate((
            (cot, held),
            (domain_hbm, domain),
            (feat.at[0:SHIFT], rows_out.at[0]),
            (feat.at[SHIFT:WIN, 0:WIN], right_out.at[0]),
            (feat.at[0:SHIFT, 0:WIN], corner_out.at[0]),
            (wqkv_hbm, wqkv),
            (wproj_hbm, wproj),
            (gain_hbm, gain),
        ))
    ]
    for copy in copies:
        copy.start()
    copies[0].wait()
    copies[1].wait()
    masks = domain_rows(domain, range(WIN), channels)
    for i in range(SHIFT):
        masked = held[i].astype(F32) * masks[i]
        rows_out[1, i] = masked.astype(BF16)
        corner_out[1, i] = masked[0:WIN].astype(BF16)
        edge = held[SHIFT + i, 0:WIN, :].astype(F32) * masks[SHIFT + i][0:WIN]
        right_out[1, i] = edge.astype(BF16)
    for copy in copies[2:]:
        copy.wait()


def block_kernel(
    feat, cot, domain, below, right, corner, wqkv, wproj, gain,
    keep, send, att_keep, att_send, dn_keep, dn_send,
    buf, shifted, projected, dattended, dcontext, context, dprojected, grads,
):
    tile_rows, cols, channels = feat.shape
    windows = cols // WIN
    cells = WIN * WIN
    half = channels // 2
    group_heads = HEADS // 2
    head_dim = channels // HEADS

    assemble_shifted(buf, feat[SHIFT:WIN].astype(F32), below.at[0], right.at[0], corner.at[0])
    for w in range(windows):
        x = buf[:, SHIFT + WIN * w : SHIFT + WIN * (w + 1), :].reshape(cells, channels)
        centred = x - jnp.mean(x, -1, keepdims=True)
        variance = jnp.mean(centred * centred, -1, keepdims=True)
        normed = centred * lax.rsqrt(variance + NORM_EPSILON) * gain[...]
        shifted[cells * w : cells * (w + 1), :] = normed.astype(BF16)

    masks = domain_rows(domain, range(SHIFT, WIN), channels)
    own = jnp.stack([cot[SHIFT + i].astype(F32) * masks[i] for i in range(SHIFT)], 0)
    assemble_shifted(buf, own, below.at[1], right.at[1], corner.at[1])
    for w in range(windows):
        x = buf[:, SHIFT + WIN * w : SHIFT + WIN * (w + 1), :].reshape(cells, channels)
        dattended[cells * w : cells * (w + 1), :] = x.astype(BF16)

    step = 128
    for m in range(0, cells * windows, step):
        projected[m : m + step, :] = dot(shifted[m : m + step, :], wqkv[...], 1, 0).astype(BF16)
        dcontext[m : m + step, :] = dot(dattended[m : m + step, :], wproj[...], 1, 1).astype(BF16)

    last_row = lax.axis_index("row") == lax.axis_size("row") - 1
    last_col = lax.axis_index("col") == lax.axis_size("col") - 1
    wide = group_heads * cells
    key_id = lax.broadcasted_iota(jnp.int32, (cells, wide), 0)
    query_id = lax.broadcasted_iota(jnp.int32, (cells, wide), 1)
    row_apart = ((key_id ^ query_id) & (WIN * SHIFT)) != 0
    col_apart = ((key_id ^ query_id) & SHIFT) != 0
    lane = lax.broadcasted_iota(jnp.int32, (cells, half), 1)
    in_head = [lane // head_dim == h for h in range(group_heads)]
    scale = head_dim ** (-0.5)

    def spread(values):
        zero = jnp.zeros_like(values)
        return jnp.concatenate([jnp.where(m, values, zero) for m in in_head], 0)

    def gather(full):
        parts = [full[cells * h : cells * (h + 1)] for h in range(group_heads)]
        out = parts[-1]
        for h in range(group_heads - 2, -1, -1):
            out = jnp.where(in_head[h], parts[h], out)
        return out

    def one_window(base, excluded):
        for g in range(2):
            at = half * g
            rows = pl.ds(base, cells)
            query = projected[rows, at : at + half]
            key = projected[rows, channels + at : channels + at + half]
            value = projected[rows, 2 * channels + at : 2 * channels + at + half]
            dctx = dcontext[rows, at : at + half]
            query_x = spread(query)
            dctx_x = spread(dctx)
            scores = dot(key, query_x, 1, 1)
            scores = jnp.where(excluded, MASKED_SCORE, scores)
            peak = jnp.max(scores, 0, keepdims=True)
            weights = jnp.exp2((scores - peak) * (scale * LOG2_E))
            probability = weights * (1.0 / jnp.sum(weights, 0, keepdims=True))
            prob16 = probability.astype(BF16)
            context[rows, at : at + half] = gather(dot(prob16, value, 0, 0)).astype(BF16)
            dprob = dot(value, dctx_x, 1, 1).astype(BF16).astype(F32)
            mean = jnp.sum(probability * dprob, 0, keepdims=True)
            dscore = (probability * (dprob - mean) * scale).astype(BF16)
            dprojected[rows, at : at + half] = gather(dot(dscore, key, 0, 0)).astype(BF16)
            dprojected[rows, channels + at : channels + at + half] = dot(
                dscore, query_x, 1, 0
            ).astype(BF16)
            dprojected[rows, 2 * channels + at : 2 * channels + at + half] = dot(
                prob16, dctx_x, 1, 0
            ).astype(BF16)

    row_excluded = jnp.logical_and(row_apart, last_row)
    for w in range(windows):
        excluded = row_excluded
        if w == windows - 1:
            excluded = jnp.logical_or(excluded, jnp.logical_and(col_apart, last_col))
        one_window(cells * w, excluded)

    for b in range(3):
        grads[channels * b : channels * (b + 1), :] = dot(
            shifted[...], dprojected[:, channels * b : channels * (b + 1)], 0, 0
        ).astype(BF16)
    grads[3 * channels : 4 * channels, :] = dot(context[...], dattended[...], 0, 0).astype(BF16)
    mine = lax.axis_index("col")
    keep[...] = grads[pl.ds(pl.multiple_of(mine * 2 * channels, 2 * channels), 2 * channels), :]
    send[...] = grads[
        pl.ds(pl.multiple_of((1 - mine) * 2 * channels, 2 * channels), 2 * channels), :
    ]

    def leave(stay, go):
        stay[...] = buf[0:SHIFT, 0:cols, :].astype(BF16)
        go[...] = buf[SHIFT:WIN, 0:cols, :].astype(BF16)

    for w in range(windows):
        rows = slice(cells * w, cells * (w + 1))
        buf[:, WIN * w : WIN * (w + 1), :] = dot(context[rows, :], wproj[...], 1, 0).reshape(
            WIN, WIN, channels
        )
    leave(att_keep, att_send)
    for w in range(windows):
        rows = slice(cells * w, cells * (w + 1))
        buf[:, WIN * w : WIN * (w + 1), :] = dot(dprojected[rows, :], wqkv[...], 1, 1).reshape(
            WIN, WIN, channels
        )
    leave(dn_keep, dn_send)


def finish_kernel(
    feat, cot, domain, gain, att_keep, att_rows, dn_keep, dn_rows, edges,
    updated, grad_features,
    buf,
):
    tile_rows, cols, channels = feat.shape
    masks = domain_rows(domain, range(WIN), channels)

    def unshifted(slot, stayed, came):
        buf[0:SHIFT, 0:WIN, :] = edges[2 * slot].astype(F32)
        buf[SHIFT:WIN, 0:WIN, :] = edges[2 * slot + 1].astype(F32)
        buf[0:SHIFT, WIN : WIN + cols, :] = came[...].astype(F32)
        buf[SHIFT:WIN, WIN : WIN + cols, :] = stayed[...].astype(F32)

    unshifted(0, att_keep, att_rows)
    for i in range(WIN):
        back = buf[i, SHIFT : SHIFT + cols, :]
        updated[i] = (feat[i].astype(F32) + masks[i] * back).astype(BF16)
    unshifted(1, dn_keep, dn_rows)
    for i in range(WIN):
        upstream = buf[i, SHIFT : SHIFT + cols, :] * gain[...]
        x = feat[i].astype(F32)
        centred = x - jnp.mean(x, -1, keepdims=True)
        variance = jnp.mean(centred * centred, -1, keepdims=True)
        inverse = lax.rsqrt(variance + NORM_EPSILON)
        standard = centred * inverse
        along = jnp.mean(upstream * standard, -1, keepdims=True)
        flat = jnp.mean(upstream, -1, keepdims=True)
        grad = inverse * (upstream - flat - standard * along)
        grad_features[i] = (cot[i].astype(F32) + grad).astype(BF16)


def sums_kernel(own, row_peer, col_peer, wqkv, gain, grad_qkv, grad_proj, grad_gain, blocks):
    channels = own.shape[0]
    mine_col = lax.axis_index("col")
    mine_row = lax.axis_index("row") % 2
    blocks[2 * mine_col + mine_row] = own[...].astype(F32)
    blocks[2 * mine_col + 1 - mine_row] = row_peer[...].astype(F32)
    other = 2 * (1 - mine_col)
    blocks[other] = col_peer[0:channels, :].astype(F32)
    blocks[other + 1] = col_peer[channels:, :].astype(F32)
    total = jnp.zeros((8, channels), F32)
    ones = jnp.ones((8, channels), BF16)
    for b in range(3):
        part = blocks[b]
        grad_qkv[:, channels * b : channels * (b + 1)] = part
        product = part * wqkv[:, channels * b : channels * (b + 1)].astype(F32)
        high = product.astype(BF16)
        low = (product - high.astype(F32)).astype(BF16)
        total = total + dot(ones, high, 1, 1) + dot(ones, low, 1, 1)
    grad_proj[...] = blocks[3]
    grad_gain[...] = total[0:1, :] / gain[...]


VMEM = pl.BlockSpec(memory_space=pltpu.MemorySpace.VMEM)
HBM = pl.BlockSpec(memory_space=pltpu.MemorySpace.HBM)


def run(kernel, out_shapes, scratch, *operands, unstaged=()):
    operands = [
        pltpu.with_memory_space_constraint(a, pltpu.MemorySpace.HBM) if i in unstaged else a
        for i, a in enumerate(operands)
    ]
    return pl.pallas_call(
        kernel,
        out_shape=out_shapes,
        in_specs=[HBM if i in unstaged else VMEM for i in range(len(operands))],
        scratch_shapes=scratch,
        compiler_params=pltpu.CompilerParams(vmem_limit_bytes=48 << 20),
    )(*operands)


def ahead(array, axes):
    sizes = [lax.axis_size(a) for a in axes]
    if len(axes) == 1:
        pairs = [(i, (i - 1) % sizes[0]) for i in range(sizes[0])]
    else:
        rows, cols = sizes
        pairs = [
            (r * cols + c, (r - 1) % rows * cols + (c - 1) % cols)
            for r in range(rows)
            for c in range(cols)
        ]
    return lax.ppermute(array, axes if len(axes) > 1 else axes[0], pairs)


def behind(array, axis):
    peers = lax.axis_size(axis)
    return lax.ppermute(array, axis, [(i, (i + 1) % peers) for i in range(peers)])


def swap(array, axis, bit):
    return lax.ppermute(array, axis, [(i, i ^ bit) for i in range(lax.axis_size(axis))])


def add16(left, right):
    return (left.astype(F32) + right.astype(F32)).astype(BF16)


def on_device(features, cotangent, domain, qkv_weight, proj_weight, norm_gain):
    tile_rows, cols, channels = features.shape
    gain = norm_gain.reshape(1, channels)
    tokens = tile_rows * cols

    def shape(dims, dtype):
        return jax.ShapeDtypeStruct(dims, dtype)

    rows_out, right_out, corner_out, cotangent, domain, qkv_weight, proj_weight, gain = run(
        pack_kernel,
        (
            shape((2, SHIFT, cols, channels), BF16),
            shape((2, SHIFT, WIN, channels), BF16),
            shape((2, SHIFT, WIN, channels), BF16),
            shape(cotangent.shape, cotangent.dtype),
            shape(domain.shape, domain.dtype),
            shape(qkv_weight.shape, qkv_weight.dtype),
            shape(proj_weight.shape, proj_weight.dtype),
            shape(gain.shape, gain.dtype),
        ),
        [pltpu.SemaphoreType.DMA((8,))],
        features, cotangent, domain, qkv_weight, proj_weight, gain,
        unstaged=(0, 1, 2, 3, 4, 5),
    )
    below = ahead(rows_out, ("row",))
    right = ahead(right_out, ("col",))
    corner = ahead(corner_out, ("row", "col"))

    strip = shape((SHIFT, cols, channels), BF16)
    keep, send, att_keep, att_send, dn_keep, dn_send = run(
        block_kernel,
        (
            shape((2 * channels, channels), BF16),
            shape((2 * channels, channels), BF16),
            strip,
            strip,
            strip,
            strip,
        ),
        [
            pltpu.VMEM((WIN, cols + WIN, channels), F32),
            pltpu.VMEM((tokens, channels), BF16),
            pltpu.VMEM((tokens, 3 * channels), BF16),
            pltpu.VMEM((tokens, channels), BF16),
            pltpu.VMEM((tokens, channels), BF16),
            pltpu.VMEM((tokens, channels), BF16),
            pltpu.VMEM((tokens, 3 * channels), BF16),
            pltpu.VMEM((4 * channels, channels), BF16),
        ],
        features, cotangent, domain, below, right, corner, qkv_weight, proj_weight, gain,
    )
    att_rows = behind(att_send, "row")
    dn_rows = behind(dn_send, "row")

    summed = add16(keep, swap(send, "col", 1))
    mine_row = lax.axis_index("row") % 2
    mine = lax.dynamic_slice_in_dim(summed, mine_row * channels, channels, 0)
    other = lax.dynamic_slice_in_dim(summed, (1 - mine_row) * channels, channels, 0)
    own = add16(mine, swap(other, "row", 1))
    bit = 2
    while bit < lax.axis_size("row"):
        if bit == 4:
            own, att_rows = lax.optimization_barrier((own, att_rows))
        own = add16(own, swap(own, "row", bit))
        bit *= 2
    own, dn_rows = lax.optimization_barrier((own, dn_rows))
    edges = jnp.stack(
        [part[:, cols - WIN :] for part in (att_rows, att_keep, dn_rows, dn_keep)], 0
    )
    edges = behind(edges, "col")
    row_peer = swap(own, "row", 1)
    pair = jnp.where(
        mine_row == 0,
        jnp.concatenate([own, row_peer], 0),
        jnp.concatenate([row_peer, own], 0),
    )
    updated, grad_features = run(
        finish_kernel,
        (shape(features.shape, BF16), shape(features.shape, BF16)),
        [pltpu.VMEM((WIN, cols + WIN, channels), F32)],
        features, cotangent, domain, gain, att_keep, att_rows, dn_keep, dn_rows, edges,
    )
    pair, updated, grad_features = lax.optimization_barrier((pair, updated, grad_features))
    col_peer = swap(pair, "col", 1)
    grad_qkv, grad_proj, grad_gain = run(
        sums_kernel,
        (
            shape((channels, 3 * channels), F32),
            shape((channels, channels), F32),
            shape((1, channels), F32),
        ),
        [pltpu.VMEM((4, channels, channels), F32)],
        own, row_peer, col_peer, qkv_weight, gain,
    )

    return updated, grad_features, grad_qkv, grad_proj, grad_gain.reshape(channels)


def solution(mesh):
    return jax.shard_map(
        on_device,
        mesh=mesh,
        in_specs=(
            P(("grp", "row"), "col", None),
            P(("grp", "row"), "col", None),
            P(("grp", "row"), "col"),
            P(),
            P(),
            P(),
        ),
        out_specs=(
            P(("grp", "row"), "col", None),
            P(("grp", "row"), "col", None),
            P("grp", None),
            P("grp", None),
            P("grp"),
        ),
        check_vma=False,
    )
```

```python
import jax
import jax.numpy as jnp
from jax import lax
from jax.experimental import pallas as pl
from jax.experimental.pallas import tpu as pltpu
from jax.sharding import PartitionSpec as P

HEADS = 8
WIN = 8
SHIFT = 4
NORM_EPSILON = 1e-05
MASKED_SCORE = -1e30
LOG2_E = 1.4426950408889634

BF16 = jnp.bfloat16
F32 = jnp.float32


def dot(left, right, left_dim, right_dim):
    return lax.dot_general(
        left, right, (((left_dim,), (right_dim,)), ((), ())), preferred_element_type=F32
    )


def assemble_shifted(buf, own, below, right, corner):
    cols = own.shape[1]
    buf[0:SHIFT, 0:cols, :] = own
    buf[SHIFT:WIN, 0:cols, :] = below[...].astype(F32)
    buf[0:SHIFT, cols : cols + WIN, :] = right[...].astype(F32)
    buf[SHIFT:WIN, cols : cols + WIN, :] = corner[...].astype(F32)


def domain_rows(domain, rows, channels):
    flags = domain[...].astype(F32).astype(BF16)
    row_ids = lax.broadcasted_iota(jnp.int32, (flags.shape[0], channels), 0)
    return [dot(flags, (row_ids == row).astype(F32).astype(BF16), 0, 0) for row in rows]


def pack_kernel(
    feat, cot, domain_hbm, wqkv_hbm, wproj_hbm, gain_hbm,
    rows_out, right_out, corner_out, held, domain, wqkv, wproj, gain,
    sems,
):
    channels = feat.shape[-1]
    copies = [
        pltpu.make_async_copy(source, target, sems.at[i])
        for i, (source, target) in enumerate((
            (cot, held),
            (domain_hbm, domain),
            (feat.at[0:SHIFT], rows_out.at[0]),
            (feat.at[SHIFT:WIN, 0:WIN], right_out.at[0]),
            (feat.at[0:SHIFT, 0:WIN], corner_out.at[0]),
            (wqkv_hbm, wqkv),
            (wproj_hbm, wproj),
            (gain_hbm, gain),
        ))
    ]
    for copy in copies:
        copy.start()
    copies[0].wait()
    copies[1].wait()
    masks = domain_rows(domain, range(WIN), channels)
    for i in range(SHIFT):
        masked = held[i].astype(F32) * masks[i]
        rows_out[1, i] = masked.astype(BF16)
        corner_out[1, i] = masked[0:WIN].astype(BF16)
        edge = held[SHIFT + i, 0:WIN, :].astype(F32) * masks[SHIFT + i][0:WIN]
        right_out[1, i] = edge.astype(BF16)
    for copy in copies[2:]:
        copy.wait()


def block_kernel(
    feat, cot, domain, below, right, corner, wqkv, wproj, gain,
    keep, send, att_keep, att_send, dn_keep, dn_send,
    buf, shifted, projected, dattended, dcontext, context, dprojected, grads,
    query_held, dctx_held, scores_held, dchances_held, chances_held, dscore_held,
):
    tile_rows, cols, channels = feat.shape
    windows = cols // WIN
    cells = WIN * WIN
    half = channels // 2
    group_heads = HEADS // 2
    head_dim = channels // HEADS

    assemble_shifted(buf, feat[SHIFT:WIN].astype(F32), below.at[0], right.at[0], corner.at[0])
    x = buf[:, SHIFT : SHIFT + cols, :]
    centred = x - jnp.mean(x, -1, keepdims=True)
    variance = jnp.mean(centred * centred, -1, keepdims=True)
    normed = centred * lax.rsqrt(variance + NORM_EPSILON) * gain[...].reshape(1, 1, channels)
    for w in range(windows):
        tile = normed[:, WIN * w : WIN * (w + 1), :].reshape(cells, channels)
        shifted[cells * w : cells * (w + 1), :] = tile.astype(BF16)

    masks = domain_rows(domain, range(SHIFT, WIN), channels)
    own = jnp.stack([cot[SHIFT + i].astype(F32) * masks[i] for i in range(SHIFT)], 0)
    assemble_shifted(buf, own, below.at[1], right.at[1], corner.at[1])
    for w in range(windows):
        x = buf[:, SHIFT + WIN * w : SHIFT + WIN * (w + 1), :].reshape(cells, channels)
        dattended[cells * w : cells * (w + 1), :] = x.astype(BF16)

    projected[...] = dot(shifted[...], wqkv[...], 1, 0).astype(BF16)
    dcontext[...] = dot(dattended[...], wproj[...], 1, 1).astype(BF16)

    last_row = lax.axis_index("row") == lax.axis_size("row") - 1
    last_col = lax.axis_index("col") == lax.axis_size("col") - 1
    wide = group_heads * cells
    key_id = lax.broadcasted_iota(jnp.int32, (cells, wide), 0)
    query_id = lax.broadcasted_iota(jnp.int32, (cells, wide), 1)
    row_apart = ((key_id ^ query_id) & (WIN * SHIFT)) != 0
    col_apart = ((key_id ^ query_id) & SHIFT) != 0
    lane = lax.broadcasted_iota(jnp.int32, (cells, half), 1)
    in_head = [lane // head_dim == h for h in range(group_heads)]
    scale = head_dim ** (-0.5)

    def spread(values):
        zero = jnp.zeros_like(values)
        return jnp.concatenate([jnp.where(m, values, zero) for m in in_head], 0)

    def gather(full):
        parts = [full[cells * h : cells * (h + 1)] for h in range(group_heads)]
        out = parts[-1]
        for h in range(group_heads - 2, -1, -1):
            out = jnp.where(in_head[h], parts[h], out)
        return out

    row_excluded = jnp.logical_and(row_apart, last_row)
    groups = [(w, g) for w in range(windows) for g in range(2)]
    depth = scores_held.shape[0]
    for first in range(0, len(groups), depth):
        batch = groups[first : first + depth]
        for n, (w, g) in enumerate(batch):
            rows = slice(cells * w, cells * (w + 1))
            at = half * g
            query_x = spread(projected[rows, at : at + half])
            key = projected[rows, channels + at : channels + at + half]
            value = projected[rows, 2 * channels + at : 2 * channels + at + half]
            dctx_x = spread(dcontext[rows, at : at + half])
            query_held[n] = query_x
            dctx_held[n] = dctx_x
            scores_held[n] = dot(key, query_x, 1, 1)
            dchances_held[n] = dot(value, dctx_x, 1, 1)
        for n, (w, g) in enumerate(batch):
            excluded = row_excluded
            if w == windows - 1:
                excluded = jnp.logical_or(excluded, jnp.logical_and(col_apart, last_col))
            scores = jnp.where(excluded, MASKED_SCORE, scores_held[n])
            peak = jnp.max(scores, 0, keepdims=True)
            weights = jnp.exp2((scores - peak) * (scale * LOG2_E))
            chances = weights * (1.0 / jnp.sum(weights, 0, keepdims=True))
            chances_held[n] = chances.astype(BF16)
            dchances = dchances_held[n].astype(BF16).astype(F32)
            mean = jnp.sum(chances * dchances, 0, keepdims=True)
            dscore_held[n] = (chances * (dchances - mean) * scale).astype(BF16)
        for n, (w, g) in enumerate(batch):
            rows = slice(cells * w, cells * (w + 1))
            at = half * g
            key = projected[rows, channels + at : channels + at + half]
            value = projected[rows, 2 * channels + at : 2 * channels + at + half]
            context[rows, at : at + half] = gather(dot(chances_held[n], value, 0, 0)).astype(BF16)
            dprojected[rows, at : at + half] = gather(dot(dscore_held[n], key, 0, 0)).astype(BF16)
            dprojected[rows, channels + at : channels + at + half] = dot(
                dscore_held[n], query_held[n], 1, 0
            ).astype(BF16)
            dprojected[rows, 2 * channels + at : 2 * channels + at + half] = dot(
                chances_held[n], dctx_held[n], 1, 0
            ).astype(BF16)

    for b in range(3):
        grads[channels * b : channels * (b + 1), :] = dot(
            shifted[...], dprojected[:, channels * b : channels * (b + 1)], 0, 0
        ).astype(BF16)
    grads[3 * channels : 4 * channels, :] = dot(context[...], dattended[...], 0, 0).astype(BF16)
    mine = lax.axis_index("col")
    keep[...] = grads[pl.ds(pl.multiple_of(mine * 2 * channels, 2 * channels), 2 * channels), :]
    send[...] = grads[
        pl.ds(pl.multiple_of((1 - mine) * 2 * channels, 2 * channels), 2 * channels), :
    ]

    full = dot(context[...], wproj[...], 1, 0)
    for w in range(windows):
        tile = full[cells * w : cells * (w + 1)].reshape(WIN, WIN, channels).astype(BF16)
        att_keep[:, WIN * w : WIN * (w + 1), :] = tile[0:SHIFT]
        att_send[:, WIN * w : WIN * (w + 1), :] = tile[SHIFT:WIN]
    full = dot(dprojected[...], wqkv[...], 1, 1)
    for w in range(windows):
        tile = full[cells * w : cells * (w + 1)].reshape(WIN, WIN, channels).astype(BF16)
        dn_keep[:, WIN * w : WIN * (w + 1), :] = tile[0:SHIFT]
        dn_send[:, WIN * w : WIN * (w + 1), :] = tile[SHIFT:WIN]


def finish_kernel(
    feat, cot, domain, gain, att_keep, att_rows, dn_keep, dn_rows, edges,
    updated, grad_features,
    buf,
):
    tile_rows, cols, channels = feat.shape
    masks = domain_rows(domain, range(WIN), channels)

    def unshifted(slot, stayed, came):
        buf[0:SHIFT, 0:WIN, :] = edges[2 * slot].astype(F32)
        buf[SHIFT:WIN, 0:WIN, :] = edges[2 * slot + 1].astype(F32)
        buf[0:SHIFT, WIN : WIN + cols, :] = came[...].astype(F32)
        buf[SHIFT:WIN, WIN : WIN + cols, :] = stayed[...].astype(F32)

    unshifted(0, att_keep, att_rows)
    for i in range(WIN):
        back = buf[i, SHIFT : SHIFT + cols, :]
        updated[i] = (feat[i].astype(F32) + masks[i] * back).astype(BF16)
    unshifted(1, dn_keep, dn_rows)
    for i in range(WIN):
        upstream = buf[i, SHIFT : SHIFT + cols, :] * gain[...]
        x = feat[i].astype(F32)
        centred = x - jnp.mean(x, -1, keepdims=True)
        variance = jnp.mean(centred * centred, -1, keepdims=True)
        inverse = lax.rsqrt(variance + NORM_EPSILON)
        standard = centred * inverse
        along = jnp.mean(upstream * standard, -1, keepdims=True)
        flat = jnp.mean(upstream, -1, keepdims=True)
        grad = inverse * (upstream - flat - standard * along)
        grad_features[i] = (cot[i].astype(F32) + grad).astype(BF16)


def sums_kernel(own, row_peer, col_peer, wqkv, gain, grad_qkv, grad_proj, grad_gain, blocks):
    channels = own.shape[0]
    mine_col = lax.axis_index("col")
    mine_row = lax.axis_index("row") % 2
    blocks[2 * mine_col + mine_row] = own[...].astype(F32)
    blocks[2 * mine_col + 1 - mine_row] = row_peer[...].astype(F32)
    other = 2 * (1 - mine_col)
    blocks[other] = col_peer[0:channels, :].astype(F32)
    blocks[other + 1] = col_peer[channels:, :].astype(F32)
    total = jnp.zeros((8, channels), F32)
    ones = jnp.ones((8, channels), BF16)
    for b in range(3):
        part = blocks[b]
        grad_qkv[:, channels * b : channels * (b + 1)] = part
        product = part * wqkv[:, channels * b : channels * (b + 1)].astype(F32)
        high = product.astype(BF16)
        low = (product - high.astype(F32)).astype(BF16)
        total = total + dot(ones, high, 1, 1) + dot(ones, low, 1, 1)
    grad_proj[...] = blocks[3]
    grad_gain[...] = total[0:1, :] / gain[...]


VMEM = pl.BlockSpec(memory_space=pltpu.MemorySpace.VMEM)
HBM = pl.BlockSpec(memory_space=pltpu.MemorySpace.HBM)


def run(kernel, out_shapes, scratch, *operands, unstaged=()):
    operands = [
        pltpu.with_memory_space_constraint(a, pltpu.MemorySpace.HBM) if i in unstaged else a
        for i, a in enumerate(operands)
    ]
    return pl.pallas_call(
        kernel,
        out_shape=out_shapes,
        in_specs=[HBM if i in unstaged else VMEM for i in range(len(operands))],
        scratch_shapes=scratch,
        compiler_params=pltpu.CompilerParams(vmem_limit_bytes=48 << 20),
    )(*operands)


def ahead(array, axes):
    sizes = [lax.axis_size(a) for a in axes]
    if len(axes) == 1:
        pairs = [(i, (i - 1) % sizes[0]) for i in range(sizes[0])]
    else:
        rows, cols = sizes
        pairs = [
            (r * cols + c, (r - 1) % rows * cols + (c - 1) % cols)
            for r in range(rows)
            for c in range(cols)
        ]
    return lax.ppermute(array, axes if len(axes) > 1 else axes[0], pairs)


def behind(array, axis):
    peers = lax.axis_size(axis)
    return lax.ppermute(array, axis, [(i, (i + 1) % peers) for i in range(peers)])


def swap(array, axis, bit):
    return lax.ppermute(array, axis, [(i, i ^ bit) for i in range(lax.axis_size(axis))])


def add16(left, right):
    return (left.astype(F32) + right.astype(F32)).astype(BF16)


def on_device(features, cotangent, domain, qkv_weight, proj_weight, norm_gain):
    tile_rows, cols, channels = features.shape
    gain = norm_gain.reshape(1, channels)
    tokens = tile_rows * cols

    def shape(dims, dtype):
        return jax.ShapeDtypeStruct(dims, dtype)

    rows_out, right_out, corner_out, cotangent, domain, qkv_weight, proj_weight, gain = run(
        pack_kernel,
        (
            shape((2, SHIFT, cols, channels), BF16),
            shape((2, SHIFT, WIN, channels), BF16),
            shape((2, SHIFT, WIN, channels), BF16),
            shape(cotangent.shape, cotangent.dtype),
            shape(domain.shape, domain.dtype),
            shape(qkv_weight.shape, qkv_weight.dtype),
            shape(proj_weight.shape, proj_weight.dtype),
            shape(gain.shape, gain.dtype),
        ),
        [pltpu.SemaphoreType.DMA((8,))],
        features, cotangent, domain, qkv_weight, proj_weight, gain,
        unstaged=(0, 1, 2, 3, 4, 5),
    )
    below = ahead(rows_out, ("row",))
    right = ahead(right_out, ("col",))
    corner = ahead(corner_out, ("row", "col"))

    strip = shape((SHIFT, cols, channels), BF16)
    keep, send, att_keep, att_send, dn_keep, dn_send = run(
        block_kernel,
        (
            shape((2 * channels, channels), BF16),
            shape((2 * channels, channels), BF16),
            strip,
            strip,
            strip,
            strip,
        ),
        [
            pltpu.VMEM((WIN, cols + WIN, channels), F32),
            pltpu.VMEM((tokens, channels), BF16),
            pltpu.VMEM((tokens, 3 * channels), BF16),
            pltpu.VMEM((tokens, channels), BF16),
            pltpu.VMEM((tokens, channels), BF16),
            pltpu.VMEM((tokens, channels), BF16),
            pltpu.VMEM((tokens, 3 * channels), BF16),
            pltpu.VMEM((4 * channels, channels), BF16),
            pltpu.VMEM((8, 4 * WIN * WIN, channels // 2), BF16),
            pltpu.VMEM((8, 4 * WIN * WIN, channels // 2), BF16),
            pltpu.VMEM((8, WIN * WIN, 4 * WIN * WIN), F32),
            pltpu.VMEM((8, WIN * WIN, 4 * WIN * WIN), F32),
            pltpu.VMEM((8, WIN * WIN, 4 * WIN * WIN), BF16),
            pltpu.VMEM((8, WIN * WIN, 4 * WIN * WIN), BF16),
        ],
        features, cotangent, domain, below, right, corner, qkv_weight, proj_weight, gain,
    )
    att_rows = behind(att_send, "row")
    dn_rows = behind(dn_send, "row")

    summed = add16(keep, swap(send, "col", 1))
    mine_row = lax.axis_index("row") % 2
    mine = lax.dynamic_slice_in_dim(summed, mine_row * channels, channels, 0)
    other = lax.dynamic_slice_in_dim(summed, (1 - mine_row) * channels, channels, 0)
    own = add16(mine, swap(other, "row", 1))
    bit = 2
    while bit < lax.axis_size("row"):
        if bit == 4:
            own, att_rows = lax.optimization_barrier((own, att_rows))
        own = add16(own, swap(own, "row", bit))
        bit *= 2
    own, dn_rows = lax.optimization_barrier((own, dn_rows))
    edges = jnp.stack(
        [part[:, cols - WIN :] for part in (att_rows, att_keep, dn_rows, dn_keep)], 0
    )
    edges = behind(edges, "col")
    row_peer = swap(own, "row", 1)
    pair = jnp.where(
        mine_row == 0,
        jnp.concatenate([own, row_peer], 0),
        jnp.concatenate([row_peer, own], 0),
    )
    updated, grad_features = run(
        finish_kernel,
        (shape(features.shape, BF16), shape(features.shape, BF16)),
        [pltpu.VMEM((WIN, cols + WIN, channels), F32)],
        features, cotangent, domain, gain, att_keep, att_rows, dn_keep, dn_rows, edges,
    )
    pair, updated, grad_features = lax.optimization_barrier((pair, updated, grad_features))
    col_peer = swap(pair, "col", 1)
    grad_qkv, grad_proj, grad_gain = run(
        sums_kernel,
        (
            shape((channels, 3 * channels), F32),
            shape((channels, channels), F32),
            shape((1, channels), F32),
        ),
        [pltpu.VMEM((4, channels, channels), F32)],
        own, row_peer, col_peer, qkv_weight, gain,
    )

    return updated, grad_features, grad_qkv, grad_proj, grad_gain.reshape(channels)


def solution(mesh):
    return jax.shard_map(
        on_device,
        mesh=mesh,
        in_specs=(
            P(("grp", "row"), "col", None),
            P(("grp", "row"), "col", None),
            P(("grp", "row"), "col"),
            P(),
            P(),
            P(),
        ),
        out_specs=(
            P(("grp", "row"), "col", None),
            P(("grp", "row"), "col", None),
            P("grp", None),
            P("grp", None),
            P("grp"),
        ),
        check_vma=False,
    )
```

```python
import jax
import jax.numpy as jnp
from jax import lax
from jax.experimental import pallas as pl
from jax.experimental.pallas import tpu as pltpu
from jax.sharding import PartitionSpec as P

HEADS = 8
WIN = 8
SHIFT = 4
NORM_EPSILON = 1e-05
MASKED_SCORE = -1e30
LOG2_E = 1.4426950408889634

BF16 = jnp.bfloat16
F32 = jnp.float32


def dot(left, right, left_dim, right_dim):
    return lax.dot_general(
        left, right, (((left_dim,), (right_dim,)), ((), ())), preferred_element_type=F32
    )


def assemble_shifted(buf, own, below, right, corner):
    cols = own.shape[1]
    buf[0:SHIFT, 0:cols, :] = own
    buf[SHIFT:WIN, 0:cols, :] = below[...].astype(F32)
    buf[0:SHIFT, cols : cols + WIN, :] = right[...].astype(F32)
    buf[SHIFT:WIN, cols : cols + WIN, :] = corner[...].astype(F32)


def domain_rows(domain, rows, channels):
    flags = domain[...].astype(F32).astype(BF16)
    row_ids = lax.broadcasted_iota(jnp.int32, (flags.shape[0], channels), 0)
    return [dot(flags, (row_ids == row).astype(F32).astype(BF16), 0, 0) for row in rows]


def pack_kernel(
    feat, cot, domain_hbm, wqkv_hbm, wproj_hbm, gain_hbm,
    rows_out, right_out, corner_out, held, domain, wqkv, wproj, gain,
    sems,
):
    channels = feat.shape[-1]
    copies = [
        pltpu.make_async_copy(source, target, sems.at[i])
        for i, (source, target) in enumerate((
            (domain_hbm, domain),
            (cot, held),
            (feat.at[0:SHIFT], rows_out.at[0]),
            (feat.at[SHIFT:WIN, 0:WIN], right_out.at[0]),
            (feat.at[0:SHIFT, 0:WIN], corner_out.at[0]),
            (wqkv_hbm, wqkv),
            (wproj_hbm, wproj),
            (gain_hbm, gain),
        ))
    ]
    for copy in copies:
        copy.start()
    copies[0].wait()
    masks = domain_rows(domain, range(WIN), channels)
    copies[1].wait()
    for i in range(SHIFT):
        masked = held[i].astype(F32) * masks[i]
        rows_out[1, i] = masked.astype(BF16)
        corner_out[1, i] = masked[0:WIN].astype(BF16)
        edge = held[SHIFT + i, 0:WIN, :].astype(F32) * masks[SHIFT + i][0:WIN]
        right_out[1, i] = edge.astype(BF16)
    for copy in copies[2:]:
        copy.wait()


def block_kernel(
    feat, cot, domain, below, right, corner, wqkv, wproj, gain,
    keep, send, att_keep, att_send, dn_keep, dn_send,
    buf, shifted, projected, dattended, dcontext, context, dprojected, grads,
    query_held, dctx_held, scores_held, dchances_held, chances_held, dscore_held,
):
    tile_rows, cols, channels = feat.shape
    windows = cols // WIN
    cells = WIN * WIN
    half = channels // 2
    group_heads = HEADS // 2
    head_dim = channels // HEADS

    assemble_shifted(buf, feat[SHIFT:WIN].astype(F32), below.at[0], right.at[0], corner.at[0])
    x = buf[:, SHIFT : SHIFT + cols, :]
    centred = x - jnp.mean(x, -1, keepdims=True)
    variance = jnp.mean(centred * centred, -1, keepdims=True)
    normed = centred * lax.rsqrt(variance + NORM_EPSILON) * gain[...].reshape(1, 1, channels)
    for w in range(windows):
        tile = normed[:, WIN * w : WIN * (w + 1), :].reshape(cells, channels)
        shifted[cells * w : cells * (w + 1), :] = tile.astype(BF16)

    masks = domain_rows(domain, range(SHIFT, WIN), channels)
    own = jnp.stack([cot[SHIFT + i].astype(F32) * masks[i] for i in range(SHIFT)], 0)
    assemble_shifted(buf, own, below.at[1], right.at[1], corner.at[1])
    for w in range(windows):
        x = buf[:, SHIFT + WIN * w : SHIFT + WIN * (w + 1), :].reshape(cells, channels)
        dattended[cells * w : cells * (w + 1), :] = x.astype(BF16)

    projected[...] = dot(shifted[...], wqkv[...], 1, 0).astype(BF16)
    dcontext[...] = dot(dattended[...], wproj[...], 1, 1).astype(BF16)

    last_row = lax.axis_index("row") == lax.axis_size("row") - 1
    last_col = lax.axis_index("col") == lax.axis_size("col") - 1
    wide = group_heads * cells
    key_id = lax.broadcasted_iota(jnp.int32, (cells, wide), 0)
    query_id = lax.broadcasted_iota(jnp.int32, (cells, wide), 1)
    row_apart = ((key_id ^ query_id) & (WIN * SHIFT)) != 0
    col_apart = ((key_id ^ query_id) & SHIFT) != 0
    lane = lax.broadcasted_iota(jnp.int32, (cells, half), 1)
    in_head = [lane // head_dim == h for h in range(group_heads)]
    scale = head_dim ** (-0.5)

    def spread(values):
        zero = jnp.zeros_like(values)
        return jnp.concatenate([jnp.where(m, values, zero) for m in in_head], 0)

    def gather(full):
        parts = [full[cells * h : cells * (h + 1)] for h in range(group_heads)]
        out = parts[-1]
        for h in range(group_heads - 2, -1, -1):
            out = jnp.where(in_head[h], parts[h], out)
        return out

    row_excluded = jnp.logical_and(row_apart, last_row)
    groups = [(w, g) for w in range(windows) for g in range(2)]
    depth = scores_held.shape[0]
    for first in range(0, len(groups), depth):
        batch = groups[first : first + depth]
        for n, (w, g) in enumerate(batch):
            rows = slice(cells * w, cells * (w + 1))
            at = half * g
            query_x = spread(projected[rows, at : at + half])
            key = projected[rows, channels + at : channels + at + half]
            value = projected[rows, 2 * channels + at : 2 * channels + at + half]
            dctx_x = spread(dcontext[rows, at : at + half])
            query_held[n] = query_x
            dctx_held[n] = dctx_x
            scores_held[n] = dot(key, query_x, 1, 1)
            dchances_held[n] = dot(value, dctx_x, 1, 1)
        for n, (w, g) in enumerate(batch):
            excluded = row_excluded
            if w == windows - 1:
                excluded = jnp.logical_or(excluded, jnp.logical_and(col_apart, last_col))
            scores = jnp.where(excluded, MASKED_SCORE, scores_held[n])
            peak = jnp.max(scores, 0, keepdims=True)
            weights = jnp.exp2((scores - peak) * (scale * LOG2_E))
            chances = weights * (1.0 / jnp.sum(weights, 0, keepdims=True))
            chances_held[n] = chances.astype(BF16)
            dchances = dchances_held[n].astype(BF16).astype(F32)
            mean = jnp.sum(chances * dchances, 0, keepdims=True)
            dscore_held[n] = (chances * (dchances - mean) * scale).astype(BF16)
        for n, (w, g) in enumerate(batch):
            rows = slice(cells * w, cells * (w + 1))
            at = half * g
            key = projected[rows, channels + at : channels + at + half]
            value = projected[rows, 2 * channels + at : 2 * channels + at + half]
            context[rows, at : at + half] = gather(dot(chances_held[n], value, 0, 0)).astype(BF16)
            dprojected[rows, at : at + half] = gather(dot(dscore_held[n], key, 0, 0)).astype(BF16)
            dprojected[rows, channels + at : channels + at + half] = dot(
                dscore_held[n], query_held[n], 1, 0
            ).astype(BF16)
            dprojected[rows, 2 * channels + at : 2 * channels + at + half] = dot(
                chances_held[n], dctx_held[n], 1, 0
            ).astype(BF16)

    for b in range(3):
        grads[channels * b : channels * (b + 1), :] = dot(
            shifted[...], dprojected[:, channels * b : channels * (b + 1)], 0, 0
        ).astype(BF16)
    grads[3 * channels : 4 * channels, :] = dot(context[...], dattended[...], 0, 0).astype(BF16)
    mine = lax.axis_index("col")
    keep[...] = grads[pl.ds(pl.multiple_of(mine * 2 * channels, 2 * channels), 2 * channels), :]
    send[...] = grads[
        pl.ds(pl.multiple_of((1 - mine) * 2 * channels, 2 * channels), 2 * channels), :
    ]

    full = dot(context[...], wproj[...], 1, 0)
    for w in range(windows):
        tile = full[cells * w : cells * (w + 1)].reshape(WIN, WIN, channels).astype(BF16)
        att_keep[:, WIN * w : WIN * (w + 1), :] = tile[0:SHIFT]
        att_send[:, WIN * w : WIN * (w + 1), :] = tile[SHIFT:WIN]
    full = dot(dprojected[...], wqkv[...], 1, 1)
    for w in range(windows):
        tile = full[cells * w : cells * (w + 1)].reshape(WIN, WIN, channels).astype(BF16)
        dn_keep[:, WIN * w : WIN * (w + 1), :] = tile[0:SHIFT]
        dn_send[:, WIN * w : WIN * (w + 1), :] = tile[SHIFT:WIN]


def finish_kernel(
    feat, cot, domain, gain, att_keep, att_rows, dn_keep, dn_rows, edges,
    updated, grad_features,
    buf,
):
    tile_rows, cols, channels = feat.shape
    masks = domain_rows(domain, range(WIN), channels)

    def unshifted(slot, stayed, came):
        buf[0:SHIFT, 0:WIN, :] = edges[2 * slot].astype(F32)
        buf[SHIFT:WIN, 0:WIN, :] = edges[2 * slot + 1].astype(F32)
        buf[0:SHIFT, WIN : WIN + cols, :] = came[...].astype(F32)
        buf[SHIFT:WIN, WIN : WIN + cols, :] = stayed[...].astype(F32)

    unshifted(0, att_keep, att_rows)
    for i in range(WIN):
        back = buf[i, SHIFT : SHIFT + cols, :]
        updated[i] = (feat[i].astype(F32) + masks[i] * back).astype(BF16)
    unshifted(1, dn_keep, dn_rows)
    for i in range(WIN):
        upstream = buf[i, SHIFT : SHIFT + cols, :] * gain[...]
        x = feat[i].astype(F32)
        centred = x - jnp.mean(x, -1, keepdims=True)
        variance = jnp.mean(centred * centred, -1, keepdims=True)
        inverse = lax.rsqrt(variance + NORM_EPSILON)
        standard = centred * inverse
        along = jnp.mean(upstream * standard, -1, keepdims=True)
        flat = jnp.mean(upstream, -1, keepdims=True)
        grad = inverse * (upstream - flat - standard * along)
        grad_features[i] = (cot[i].astype(F32) + grad).astype(BF16)


def sums_kernel(half, col_peer, wqkv, gain, grad_qkv, grad_proj, grad_gain, halves):
    channels = wqkv.shape[0]
    mine = lax.axis_index("col")
    halves[mine] = half[...].astype(F32)
    halves[1 - mine] = col_peer[...].astype(F32)
    total = jnp.zeros((8, channels), F32)
    ones = jnp.ones((8, channels), BF16)
    for b in range(3):
        part = halves[b // 2, channels * (b % 2) : channels * (b % 2 + 1), :]
        grad_qkv[:, channels * b : channels * (b + 1)] = part
        product = part * wqkv[:, channels * b : channels * (b + 1)].astype(F32)
        high = product.astype(BF16)
        low = (product - high.astype(F32)).astype(BF16)
        total = total + dot(ones, high, 1, 1) + dot(ones, low, 1, 1)
    grad_proj[...] = halves[1, channels:, :]
    grad_gain[...] = total[0:1, :] / gain[...]


VMEM = pl.BlockSpec(memory_space=pltpu.MemorySpace.VMEM)
HBM = pl.BlockSpec(memory_space=pltpu.MemorySpace.HBM)


def run(kernel, out_shapes, scratch, *operands, unstaged=()):
    operands = [
        pltpu.with_memory_space_constraint(a, pltpu.MemorySpace.HBM) if i in unstaged else a
        for i, a in enumerate(operands)
    ]
    return pl.pallas_call(
        kernel,
        out_shape=out_shapes,
        in_specs=[HBM if i in unstaged else VMEM for i in range(len(operands))],
        scratch_shapes=scratch,
        compiler_params=pltpu.CompilerParams(vmem_limit_bytes=48 << 20),
    )(*operands)


def ahead(array, axes):
    sizes = [lax.axis_size(a) for a in axes]
    if len(axes) == 1:
        pairs = [(i, (i - 1) % sizes[0]) for i in range(sizes[0])]
    else:
        rows, cols = sizes
        pairs = [
            (r * cols + c, (r - 1) % rows * cols + (c - 1) % cols)
            for r in range(rows)
            for c in range(cols)
        ]
    return lax.ppermute(array, axes if len(axes) > 1 else axes[0], pairs)


def behind(array, axis):
    peers = lax.axis_size(axis)
    return lax.ppermute(array, axis, [(i, (i + 1) % peers) for i in range(peers)])


def swap(array, axis, bit):
    return lax.ppermute(array, axis, [(i, i ^ bit) for i in range(lax.axis_size(axis))])


def add16(left, right):
    return (left.astype(F32) + right.astype(F32)).astype(BF16)


def on_device(features, cotangent, domain, qkv_weight, proj_weight, norm_gain):
    tile_rows, cols, channels = features.shape
    gain = norm_gain.reshape(1, channels)
    tokens = tile_rows * cols

    def shape(dims, dtype):
        return jax.ShapeDtypeStruct(dims, dtype)

    rows_out, right_out, corner_out, cotangent, domain, qkv_weight, proj_weight, gain = run(
        pack_kernel,
        (
            shape((2, SHIFT, cols, channels), BF16),
            shape((2, SHIFT, WIN, channels), BF16),
            shape((2, SHIFT, WIN, channels), BF16),
            shape(cotangent.shape, cotangent.dtype),
            shape(domain.shape, domain.dtype),
            shape(qkv_weight.shape, qkv_weight.dtype),
            shape(proj_weight.shape, proj_weight.dtype),
            shape(gain.shape, gain.dtype),
        ),
        [pltpu.SemaphoreType.DMA((8,))],
        features, cotangent, domain, qkv_weight, proj_weight, gain,
        unstaged=(0, 1, 2, 3, 4, 5),
    )
    below = ahead(rows_out, ("row",))
    right = ahead(right_out, ("col",))
    corner = ahead(corner_out, ("row", "col"))

    strip = shape((SHIFT, cols, channels), BF16)
    keep, send, att_keep, att_send, dn_keep, dn_send = run(
        block_kernel,
        (
            shape((2 * channels, channels), BF16),
            shape((2 * channels, channels), BF16),
            strip,
            strip,
            strip,
            strip,
        ),
        [
            pltpu.VMEM((WIN, cols + WIN, channels), F32),
            pltpu.VMEM((tokens, channels), BF16),
            pltpu.VMEM((tokens, 3 * channels), BF16),
            pltpu.VMEM((tokens, channels), BF16),
            pltpu.VMEM((tokens, channels), BF16),
            pltpu.VMEM((tokens, channels), BF16),
            pltpu.VMEM((tokens, 3 * channels), BF16),
            pltpu.VMEM((4 * channels, channels), BF16),
            pltpu.VMEM((8, 4 * WIN * WIN, channels // 2), BF16),
            pltpu.VMEM((8, 4 * WIN * WIN, channels // 2), BF16),
            pltpu.VMEM((8, WIN * WIN, 4 * WIN * WIN), F32),
            pltpu.VMEM((8, WIN * WIN, 4 * WIN * WIN), F32),
            pltpu.VMEM((8, WIN * WIN, 4 * WIN * WIN), BF16),
            pltpu.VMEM((8, WIN * WIN, 4 * WIN * WIN), BF16),
        ],
        features, cotangent, domain, below, right, corner, qkv_weight, proj_weight, gain,
    )
    summed = add16(keep, swap(send, "col", 1))
    place = lax.axis_index("row") % 4
    chunk = channels // 2

    def piece(step):
        return lax.dynamic_slice_in_dim(summed, (place ^ step) * chunk, chunk, 0)

    att_rows = behind(att_send, "row")
    dn_rows = behind(dn_send, "row")
    received = [swap(piece(step), "row", step) for step in (1, 2, 3)]
    own = piece(0).astype(F32)
    for part in received:
        own = own + part.astype(F32)
    own = own.astype(BF16)
    bit = 4
    while bit < lax.axis_size("row"):
        received = swap(own, "row", bit)
        own = add16(own, received)
        bit *= 2
    own, att_rows, dn_rows = lax.optimization_barrier((own, att_rows, dn_rows))
    edges = jnp.stack(
        [part[:, cols - WIN :] for part in (att_rows, att_keep, dn_rows, dn_keep)], 0
    )
    edges = behind(edges, "col")
    half = jnp.zeros((2 * channels, channels), BF16)
    parts = [own] + [swap(own, "row", step) for step in (1, 2, 3)]
    for step, part in enumerate(parts):
        half = lax.dynamic_update_slice_in_dim(half, part, (place ^ step) * chunk, 0)
    updated, grad_features = run(
        finish_kernel,
        (shape(features.shape, BF16), shape(features.shape, BF16)),
        [pltpu.VMEM((WIN, cols + WIN, channels), F32)],
        features, cotangent, domain, gain, att_keep, att_rows, dn_keep, dn_rows, edges,
    )
    half, updated, grad_features = lax.optimization_barrier((half, updated, grad_features))
    col_peer = swap(half, "col", 1)
    grad_qkv, grad_proj, grad_gain = run(
        sums_kernel,
        (
            shape((channels, 3 * channels), F32),
            shape((channels, channels), F32),
            shape((1, channels), F32),
        ),
        [pltpu.VMEM((2, 2 * channels, channels), F32)],
        half, col_peer, qkv_weight, gain,
    )
    return updated, grad_features, grad_qkv, grad_proj, grad_gain.reshape(channels)


def solution(mesh):
    return jax.shard_map(
        on_device,
        mesh=mesh,
        in_specs=(
            P(("grp", "row"), "col", None),
            P(("grp", "row"), "col", None),
            P(("grp", "row"), "col"),
            P(),
            P(),
            P(),
        ),
        out_specs=(
            P(("grp", "row"), "col", None),
            P(("grp", "row"), "col", None),
            P("grp", None),
            P("grp", None),
            P("grp"),
        ),
        check_vma=False,
    )
```

```python
import jax
import jax.numpy as jnp
from jax import lax
from jax.experimental import pallas as pl
from jax.experimental.pallas import tpu as pltpu
from jax.sharding import PartitionSpec as P

HEADS = 8
WIN = 8
SHIFT = 4
NORM_EPSILON = 1e-05
MASKED_SCORE = -1e30
LOG2_E = 1.4426950408889634

BF16 = jnp.bfloat16
F32 = jnp.float32


def dot(left, right, left_dim, right_dim):
    return lax.dot_general(
        left, right, (((left_dim,), (right_dim,)), ((), ())), preferred_element_type=F32
    )


def assemble_shifted(buf, own, below, right, corner):
    cols = own.shape[1]
    buf[0:SHIFT, 0:cols, :] = own
    buf[SHIFT:WIN, 0:cols, :] = below[...].astype(F32)
    buf[0:SHIFT, cols : cols + WIN, :] = right[...].astype(F32)
    buf[SHIFT:WIN, cols : cols + WIN, :] = corner[...].astype(F32)


def domain_rows(domain, rows, channels):
    flags = domain[...].astype(F32).astype(BF16)
    row_ids = lax.broadcasted_iota(jnp.int32, (flags.shape[0], channels), 0)
    return [dot(flags, (row_ids == row).astype(F32).astype(BF16), 0, 0) for row in rows]


def pack_kernel(
    feat, cot, domain_hbm, wqkv_hbm, wproj_hbm, gain_hbm,
    rows_out, right_out, corner_out, held, domain, wqkv, wproj, gain,
    sems,
):
    channels = feat.shape[-1]
    copies = [
        pltpu.make_async_copy(source, target, sems.at[i])
        for i, (source, target) in enumerate((
            (domain_hbm, domain),
            (cot, held),
            (feat.at[0:SHIFT], rows_out.at[0]),
            (feat.at[SHIFT:WIN, 0:WIN], right_out.at[0]),
            (feat.at[0:SHIFT, 0:WIN], corner_out.at[0]),
            (wqkv_hbm, wqkv),
            (wproj_hbm, wproj),
            (gain_hbm, gain),
        ))
    ]
    for copy in copies:
        copy.start()
    copies[0].wait()
    masks = domain_rows(domain, range(WIN), channels)
    copies[1].wait()
    for i in range(SHIFT):
        masked = held[i].astype(F32) * masks[i]
        rows_out[1, i] = masked.astype(BF16)
        corner_out[1, i] = masked[0:WIN].astype(BF16)
        edge = held[SHIFT + i, 0:WIN, :].astype(F32) * masks[SHIFT + i][0:WIN]
        right_out[1, i] = edge.astype(BF16)
    for copy in copies[2:]:
        copy.wait()


def block_kernel(
    feat, cot, domain, below, right, corner, wqkv, wproj, gain,
    keep, send, att_keep, dn_keep, both_send,
    buf, shifted, projected, dattended, dcontext, context, dprojected, grads,
    query_held, dctx_held, scores_held, dchances_held, chances_held, dscore_held,
):
    tile_rows, cols, channels = feat.shape
    windows = cols // WIN
    cells = WIN * WIN
    half = channels // 2
    group_heads = HEADS // 2
    head_dim = channels // HEADS

    assemble_shifted(buf, feat[SHIFT:WIN].astype(F32), below.at[0], right.at[0], corner.at[0])
    x = buf[:, SHIFT : SHIFT + cols, :]
    centred = x - jnp.mean(x, -1, keepdims=True)
    variance = jnp.mean(centred * centred, -1, keepdims=True)
    normed = centred * lax.rsqrt(variance + NORM_EPSILON) * gain[...].reshape(1, 1, channels)
    for w in range(windows):
        tile = normed[:, WIN * w : WIN * (w + 1), :].reshape(cells, channels)
        shifted[cells * w : cells * (w + 1), :] = tile.astype(BF16)

    masks = domain_rows(domain, range(SHIFT, WIN), channels)
    own = jnp.stack([cot[SHIFT + i].astype(F32) * masks[i] for i in range(SHIFT)], 0)
    assemble_shifted(buf, own, below.at[1], right.at[1], corner.at[1])
    for w in range(windows):
        x = buf[:, SHIFT + WIN * w : SHIFT + WIN * (w + 1), :].reshape(cells, channels)
        dattended[cells * w : cells * (w + 1), :] = x.astype(BF16)

    projected[...] = dot(shifted[...], wqkv[...], 1, 0).astype(BF16)
    dcontext[...] = dot(dattended[...], wproj[...], 1, 1).astype(BF16)

    last_row = lax.axis_index("row") == lax.axis_size("row") - 1
    last_col = lax.axis_index("col") == lax.axis_size("col") - 1
    wide = group_heads * cells
    key_id = lax.broadcasted_iota(jnp.int32, (cells, wide), 0)
    query_id = lax.broadcasted_iota(jnp.int32, (cells, wide), 1)
    row_apart = ((key_id ^ query_id) & (WIN * SHIFT)) != 0
    col_apart = ((key_id ^ query_id) & SHIFT) != 0
    lane = lax.broadcasted_iota(jnp.int32, (cells, half), 1)
    in_head = [lane // head_dim == h for h in range(group_heads)]
    scale = head_dim ** (-0.5)

    def spread(values):
        zero = jnp.zeros_like(values)
        return jnp.concatenate([jnp.where(m, values, zero) for m in in_head], 0)

    def gather(full):
        parts = [full[cells * h : cells * (h + 1)] for h in range(group_heads)]
        out = parts[-1]
        for h in range(group_heads - 2, -1, -1):
            out = jnp.where(in_head[h], parts[h], out)
        return out

    row_excluded = jnp.logical_and(row_apart, last_row)
    groups = [(w, g) for w in range(windows) for g in range(2)]
    depth = scores_held.shape[0]
    for first in range(0, len(groups), depth):
        batch = groups[first : first + depth]
        for n, (w, g) in enumerate(batch):
            rows = slice(cells * w, cells * (w + 1))
            at = half * g
            query_x = spread(projected[rows, at : at + half])
            key = projected[rows, channels + at : channels + at + half]
            value = projected[rows, 2 * channels + at : 2 * channels + at + half]
            dctx_x = spread(dcontext[rows, at : at + half])
            query_held[n] = query_x
            dctx_held[n] = dctx_x
            scores_held[n] = dot(key, query_x, 1, 1)
            dchances_held[n] = dot(value, dctx_x, 1, 1)
        for n, (w, g) in enumerate(batch):
            excluded = row_excluded
            if w == windows - 1:
                excluded = jnp.logical_or(excluded, jnp.logical_and(col_apart, last_col))
            scores = jnp.where(excluded, MASKED_SCORE, scores_held[n])
            peak = jnp.max(scores, 0, keepdims=True)
            weights = jnp.exp2((scores - peak) * (scale * LOG2_E))
            chances = weights * (1.0 / jnp.sum(weights, 0, keepdims=True))
            chances_held[n] = chances.astype(BF16)
            dchances = dchances_held[n].astype(BF16).astype(F32)
            mean = jnp.sum(chances * dchances, 0, keepdims=True)
            dscore_held[n] = (chances * (dchances - mean) * scale).astype(BF16)
        for n, (w, g) in enumerate(batch):
            rows = slice(cells * w, cells * (w + 1))
            at = half * g
            key = projected[rows, channels + at : channels + at + half]
            value = projected[rows, 2 * channels + at : 2 * channels + at + half]
            context[rows, at : at + half] = gather(dot(chances_held[n], value, 0, 0)).astype(BF16)
            dprojected[rows, at : at + half] = gather(dot(dscore_held[n], key, 0, 0)).astype(BF16)
            dprojected[rows, channels + at : channels + at + half] = dot(
                dscore_held[n], query_held[n], 1, 0
            ).astype(BF16)
            dprojected[rows, 2 * channels + at : 2 * channels + at + half] = dot(
                chances_held[n], dctx_held[n], 1, 0
            ).astype(BF16)

    for b in range(3):
        grads[channels * b : channels * (b + 1), :] = dot(
            shifted[...], dprojected[:, channels * b : channels * (b + 1)], 0, 0
        ).astype(BF16)
    grads[3 * channels : 4 * channels, :] = dot(context[...], dattended[...], 0, 0).astype(BF16)
    mine = lax.axis_index("col")
    keep[...] = grads[pl.ds(pl.multiple_of(mine * 2 * channels, 2 * channels), 2 * channels), :]
    send[...] = grads[
        pl.ds(pl.multiple_of((1 - mine) * 2 * channels, 2 * channels), 2 * channels), :
    ]

    full = dot(context[...], wproj[...], 1, 0)
    for w in range(windows):
        tile = full[cells * w : cells * (w + 1)].reshape(WIN, WIN, channels).astype(BF16)
        att_keep[:, WIN * w : WIN * (w + 1), :] = tile[0:SHIFT]
        both_send[0, :, WIN * w : WIN * (w + 1), :] = tile[SHIFT:WIN]
    full = dot(dprojected[...], wqkv[...], 1, 1)
    for w in range(windows):
        tile = full[cells * w : cells * (w + 1)].reshape(WIN, WIN, channels).astype(BF16)
        dn_keep[:, WIN * w : WIN * (w + 1), :] = tile[0:SHIFT]
        both_send[1, :, WIN * w : WIN * (w + 1), :] = tile[SHIFT:WIN]


def finish_kernel(
    feat, cot, domain, gain, att_keep, dn_keep, both_rows, edges,
    updated, grad_features,
    buf,
):
    tile_rows, cols, channels = feat.shape
    masks = domain_rows(domain, range(WIN), channels)

    def unshifted(slot, stayed, came):
        buf[0:SHIFT, 0:WIN, :] = edges[2 * slot].astype(F32)
        buf[SHIFT:WIN, 0:WIN, :] = edges[2 * slot + 1].astype(F32)
        buf[0:SHIFT, WIN : WIN + cols, :] = came[...].astype(F32)
        buf[SHIFT:WIN, WIN : WIN + cols, :] = stayed[...].astype(F32)

    unshifted(0, att_keep, both_rows.at[0])
    for i in range(WIN):
        back = buf[i, SHIFT : SHIFT + cols, :]
        updated[i] = (feat[i].astype(F32) + masks[i] * back).astype(BF16)
    unshifted(1, dn_keep, both_rows.at[1])
    for i in range(WIN):
        upstream = buf[i, SHIFT : SHIFT + cols, :] * gain[...]
        x = feat[i].astype(F32)
        centred = x - jnp.mean(x, -1, keepdims=True)
        variance = jnp.mean(centred * centred, -1, keepdims=True)
        inverse = lax.rsqrt(variance + NORM_EPSILON)
        standard = centred * inverse
        along = jnp.mean(upstream * standard, -1, keepdims=True)
        flat = jnp.mean(upstream, -1, keepdims=True)
        grad = inverse * (upstream - flat - standard * along)
        grad_features[i] = (cot[i].astype(F32) + grad).astype(BF16)


def sums_kernel(half, col_peer, wqkv, gain, grad_qkv, grad_proj, grad_gain, halves):
    channels = wqkv.shape[0]
    mine = lax.axis_index("col")
    halves[mine] = half[...].astype(F32)
    halves[1 - mine] = col_peer[...].astype(F32)
    total = jnp.zeros((8, channels), F32)
    ones = jnp.ones((8, channels), BF16)
    for b in range(3):
        part = halves[b // 2, channels * (b % 2) : channels * (b % 2 + 1), :]
        grad_qkv[:, channels * b : channels * (b + 1)] = part
        product = part * wqkv[:, channels * b : channels * (b + 1)].astype(F32)
        high = product.astype(BF16)
        low = (product - high.astype(F32)).astype(BF16)
        total = total + dot(ones, high, 1, 1) + dot(ones, low, 1, 1)
    grad_proj[...] = halves[1, channels:, :]
    grad_gain[...] = total[0:1, :] / gain[...]


VMEM = pl.BlockSpec(memory_space=pltpu.MemorySpace.VMEM)
HBM = pl.BlockSpec(memory_space=pltpu.MemorySpace.HBM)


def run(kernel, out_shapes, scratch, *operands, unstaged=()):
    operands = [
        pltpu.with_memory_space_constraint(a, pltpu.MemorySpace.HBM) if i in unstaged else a
        for i, a in enumerate(operands)
    ]
    return pl.pallas_call(
        kernel,
        out_shape=out_shapes,
        in_specs=[HBM if i in unstaged else VMEM for i in range(len(operands))],
        scratch_shapes=scratch,
        compiler_params=pltpu.CompilerParams(vmem_limit_bytes=48 << 20),
    )(*operands)


def ahead(array, axes):
    sizes = [lax.axis_size(a) for a in axes]
    if len(axes) == 1:
        pairs = [(i, (i - 1) % sizes[0]) for i in range(sizes[0])]
    else:
        rows, cols = sizes
        pairs = [
            (r * cols + c, (r - 1) % rows * cols + (c - 1) % cols)
            for r in range(rows)
            for c in range(cols)
        ]
    return lax.ppermute(array, axes if len(axes) > 1 else axes[0], pairs)


def behind(array, axis):
    peers = lax.axis_size(axis)
    return lax.ppermute(array, axis, [(i, (i + 1) % peers) for i in range(peers)])


def swap(array, axis, bit):
    return lax.ppermute(array, axis, [(i, i ^ bit) for i in range(lax.axis_size(axis))])


def add16(left, right):
    return (left.astype(F32) + right.astype(F32)).astype(BF16)


def on_device(features, cotangent, domain, qkv_weight, proj_weight, norm_gain):
    tile_rows, cols, channels = features.shape
    gain = norm_gain.reshape(1, channels)
    tokens = tile_rows * cols

    def shape(dims, dtype):
        return jax.ShapeDtypeStruct(dims, dtype)

    rows_out, right_out, corner_out, cotangent, domain, qkv_weight, proj_weight, gain = run(
        pack_kernel,
        (
            shape((2, SHIFT, cols, channels), BF16),
            shape((2, SHIFT, WIN, channels), BF16),
            shape((2, SHIFT, WIN, channels), BF16),
            shape(cotangent.shape, cotangent.dtype),
            shape(domain.shape, domain.dtype),
            shape(qkv_weight.shape, qkv_weight.dtype),
            shape(proj_weight.shape, proj_weight.dtype),
            shape(gain.shape, gain.dtype),
        ),
        [pltpu.SemaphoreType.DMA((8,))],
        features, cotangent, domain, qkv_weight, proj_weight, gain,
        unstaged=(0, 1, 2, 3, 4, 5),
    )
    below = ahead(rows_out, ("row",))
    right = ahead(right_out, ("col",))
    corner = ahead(corner_out, ("row", "col"))

    strip = shape((SHIFT, cols, channels), BF16)
    keep, send, att_keep, dn_keep, both_send = run(
        block_kernel,
        (
            shape((2 * channels, channels), BF16),
            shape((2 * channels, channels), BF16),
            strip,
            strip,
            shape((2, SHIFT, cols, channels), BF16),
        ),
        [
            pltpu.VMEM((WIN, cols + WIN, channels), F32),
            pltpu.VMEM((tokens, channels), BF16),
            pltpu.VMEM((tokens, 3 * channels), BF16),
            pltpu.VMEM((tokens, channels), BF16),
            pltpu.VMEM((tokens, channels), BF16),
            pltpu.VMEM((tokens, channels), BF16),
            pltpu.VMEM((tokens, 3 * channels), BF16),
            pltpu.VMEM((4 * channels, channels), BF16),
            pltpu.VMEM((8, 4 * WIN * WIN, channels // 2), BF16),
            pltpu.VMEM((8, 4 * WIN * WIN, channels // 2), BF16),
            pltpu.VMEM((8, WIN * WIN, 4 * WIN * WIN), F32),
            pltpu.VMEM((8, WIN * WIN, 4 * WIN * WIN), F32),
            pltpu.VMEM((8, WIN * WIN, 4 * WIN * WIN), BF16),
            pltpu.VMEM((8, WIN * WIN, 4 * WIN * WIN), BF16),
        ],
        features, cotangent, domain, below, right, corner, qkv_weight, proj_weight, gain,
    )
    summed = add16(keep, swap(send, "col", 1))
    place = lax.axis_index("row") % 4
    chunk = channels // 2

    def piece(step):
        return lax.dynamic_slice_in_dim(summed, (place ^ step) * chunk, chunk, 0)

    both_rows = behind(both_send, "row")
    received = [swap(piece(step), "row", step) for step in (1, 2, 3)]
    own = piece(0).astype(F32)
    for part in received:
        own = own + part.astype(F32)
    own = own.astype(BF16)
    own, both_rows = lax.optimization_barrier((own, both_rows))
    bit = 4
    while bit < lax.axis_size("row"):
        received = swap(own, "row", bit)
        own = add16(own, received)
        bit *= 2
    edges = jnp.stack(
        [part[:, cols - WIN :] for part in (both_rows[0], att_keep, both_rows[1], dn_keep)], 0
    )
    edges = behind(edges, "col")
    half = jnp.zeros((2 * channels, channels), BF16)
    parts = [own] + [swap(own, "row", step) for step in (1, 2, 3)]
    for step, part in enumerate(parts):
        half = lax.dynamic_update_slice_in_dim(half, part, (place ^ step) * chunk, 0)
    updated, grad_features = run(
        finish_kernel,
        (shape(features.shape, BF16), shape(features.shape, BF16)),
        [pltpu.VMEM((WIN, cols + WIN, channels), F32)],
        features, cotangent, domain, gain, att_keep, dn_keep, both_rows, edges,
    )
    half, updated, grad_features = lax.optimization_barrier((half, updated, grad_features))
    col_peer = swap(half, "col", 1)
    grad_qkv, grad_proj, grad_gain = run(
        sums_kernel,
        (
            shape((channels, 3 * channels), F32),
            shape((channels, channels), F32),
            shape((1, channels), F32),
        ),
        [pltpu.VMEM((2, 2 * channels, channels), F32)],
        half, col_peer, qkv_weight, gain,
    )
    return updated, grad_features, grad_qkv, grad_proj, grad_gain.reshape(channels)


def solution(mesh):
    return jax.shard_map(
        on_device,
        mesh=mesh,
        in_specs=(
            P(("grp", "row"), "col", None),
            P(("grp", "row"), "col", None),
            P(("grp", "row"), "col"),
            P(),
            P(),
            P(),
        ),
        out_specs=(
            P(("grp", "row"), "col", None),
            P(("grp", "row"), "col", None),
            P("grp", None),
            P("grp", None),
            P("grp"),
        ),
        check_vma=False,
    )
```

```python
import jax
import jax.numpy as jnp
from jax import lax
from jax.experimental import pallas as pl
from jax.experimental.pallas import tpu as pltpu
from jax.sharding import PartitionSpec as P

HEADS = 8
WIN = 8
SHIFT = 4
NORM_EPSILON = 1e-05
MASKED_SCORE = -1e30
LOG2_E = 1.4426950408889634

BF16 = jnp.bfloat16
F32 = jnp.float32


def dot(left, right, left_dim, right_dim):
    return lax.dot_general(
        left, right, (((left_dim,), (right_dim,)), ((), ())), preferred_element_type=F32
    )


def assemble_shifted(buf, own, below, right, corner):
    cols = own.shape[1]
    buf[0:SHIFT, 0:cols, :] = own
    buf[SHIFT:WIN, 0:cols, :] = below[...].astype(F32)
    buf[0:SHIFT, cols : cols + WIN, :] = right[...].astype(F32)
    buf[SHIFT:WIN, cols : cols + WIN, :] = corner[...].astype(F32)


def domain_rows(domain, rows, channels):
    flags = domain[...].astype(F32).astype(BF16)
    row_ids = lax.broadcasted_iota(jnp.int32, (flags.shape[0], channels), 0)
    return [dot(flags, (row_ids == row).astype(F32).astype(BF16), 0, 0) for row in rows]


def pack_kernel(
    feat, cot, domain_hbm,
    rows_out, right_out, corner_out, held, domain,
    sems,
):
    channels = feat.shape[-1]
    copies = [
        pltpu.make_async_copy(source, target, sems.at[i])
        for i, (source, target) in enumerate((
            (domain_hbm, domain),
            (cot, held),
            (feat.at[0:SHIFT], rows_out.at[0]),
            (feat.at[SHIFT:WIN, 0:WIN], right_out.at[0]),
            (feat.at[0:SHIFT, 0:WIN], corner_out.at[0]),
        ))
    ]
    for copy in copies:
        copy.start()
    copies[0].wait()
    masks = domain_rows(domain, range(WIN), channels)
    copies[1].wait()
    for i in range(SHIFT):
        masked = held[i].astype(F32) * masks[i]
        rows_out[1, i] = masked.astype(BF16)
        corner_out[1, i] = masked[0:WIN].astype(BF16)
        edge = held[SHIFT + i, 0:WIN, :].astype(F32) * masks[SHIFT + i][0:WIN]
        right_out[1, i] = edge.astype(BF16)
    for copy in copies[2:]:
        copy.wait()


def fetch_kernel(wqkv_hbm, wproj_hbm, gain_hbm, wqkv, wproj, gain, sems):
    pairs = ((wqkv_hbm, wqkv), (wproj_hbm, wproj), (gain_hbm, gain))
    copies = [pltpu.make_async_copy(a, b, sems.at[i]) for i, (a, b) in enumerate(pairs)]
    for copy in copies:
        copy.start()
    for copy in copies:
        copy.wait()


def block_kernel(
    feat, cot, domain, below, right, corner, wqkv, wproj, gain,
    keep, send, att_keep, dn_keep, both_send,
    buf, shifted, projected, dattended, dcontext, context, dprojected, grads,
    query_held, dctx_held, scores_held, dchances_held, chances_held, dscore_held,
):
    tile_rows, cols, channels = feat.shape
    windows = cols // WIN
    cells = WIN * WIN
    half = channels // 2
    group_heads = HEADS // 2
    head_dim = channels // HEADS

    assemble_shifted(buf, feat[SHIFT:WIN].astype(F32), below.at[0], right.at[0], corner.at[0])
    x = buf[:, SHIFT : SHIFT + cols, :]
    centred = x - jnp.mean(x, -1, keepdims=True)
    variance = jnp.mean(centred * centred, -1, keepdims=True)
    normed = centred * lax.rsqrt(variance + NORM_EPSILON) * gain[...].reshape(1, 1, channels)
    for w in range(windows):
        tile = normed[:, WIN * w : WIN * (w + 1), :].reshape(cells, channels)
        shifted[cells * w : cells * (w + 1), :] = tile.astype(BF16)

    masks = domain_rows(domain, range(SHIFT, WIN), channels)
    own = jnp.stack([cot[SHIFT + i].astype(F32) * masks[i] for i in range(SHIFT)], 0)
    assemble_shifted(buf, own, below.at[1], right.at[1], corner.at[1])
    for w in range(windows):
        x = buf[:, SHIFT + WIN * w : SHIFT + WIN * (w + 1), :].reshape(cells, channels)
        dattended[cells * w : cells * (w + 1), :] = x.astype(BF16)

    projected[...] = dot(shifted[...], wqkv[...], 1, 0).astype(BF16)
    dcontext[...] = dot(dattended[...], wproj[...], 1, 1).astype(BF16)

    last_row = lax.axis_index("row") == lax.axis_size("row") - 1
    last_col = lax.axis_index("col") == lax.axis_size("col") - 1
    wide = group_heads * cells
    key_id = lax.broadcasted_iota(jnp.int32, (cells, wide), 0)
    query_id = lax.broadcasted_iota(jnp.int32, (cells, wide), 1)
    row_apart = ((key_id ^ query_id) & (WIN * SHIFT)) != 0
    col_apart = ((key_id ^ query_id) & SHIFT) != 0
    lane = lax.broadcasted_iota(jnp.int32, (cells, half), 1)
    in_head = [lane // head_dim == h for h in range(group_heads)]
    scale = head_dim ** (-0.5)

    def spread(values):
        zero = jnp.zeros_like(values)
        return jnp.concatenate([jnp.where(m, values, zero) for m in in_head], 0)

    def gather(full):
        parts = [full[cells * h : cells * (h + 1)] for h in range(group_heads)]
        out = parts[-1]
        for h in range(group_heads - 2, -1, -1):
            out = jnp.where(in_head[h], parts[h], out)
        return out

    row_excluded = jnp.logical_and(row_apart, last_row)
    groups = [(w, g) for w in range(windows) for g in range(2)]
    depth = scores_held.shape[0]
    for first in range(0, len(groups), depth):
        batch = groups[first : first + depth]
        for n, (w, g) in enumerate(batch):
            rows = slice(cells * w, cells * (w + 1))
            at = half * g
            query_x = spread(projected[rows, at : at + half])
            key = projected[rows, channels + at : channels + at + half]
            value = projected[rows, 2 * channels + at : 2 * channels + at + half]
            dctx_x = spread(dcontext[rows, at : at + half])
            query_held[n] = query_x
            dctx_held[n] = dctx_x
            scores_held[n] = dot(key, query_x, 1, 1)
            dchances_held[n] = dot(value, dctx_x, 1, 1)
        for n, (w, g) in enumerate(batch):
            excluded = row_excluded
            if w == windows - 1:
                excluded = jnp.logical_or(excluded, jnp.logical_and(col_apart, last_col))
            scores = jnp.where(excluded, MASKED_SCORE, scores_held[n])
            peak = jnp.max(scores, 0, keepdims=True)
            weights = jnp.exp2((scores - peak) * (scale * LOG2_E))
            chances = weights * (1.0 / jnp.sum(weights, 0, keepdims=True))
            chances_held[n] = chances.astype(BF16)
            dchances = dchances_held[n].astype(BF16).astype(F32)
            mean = jnp.sum(chances * dchances, 0, keepdims=True)
            dscore_held[n] = (chances * (dchances - mean) * scale).astype(BF16)
        for n, (w, g) in enumerate(batch):
            rows = slice(cells * w, cells * (w + 1))
            at = half * g
            key = projected[rows, channels + at : channels + at + half]
            value = projected[rows, 2 * channels + at : 2 * channels + at + half]
            context[rows, at : at + half] = gather(dot(chances_held[n], value, 0, 0)).astype(BF16)
            dprojected[rows, at : at + half] = gather(dot(dscore_held[n], key, 0, 0)).astype(BF16)
            dprojected[rows, channels + at : channels + at + half] = dot(
                dscore_held[n], query_held[n], 1, 0
            ).astype(BF16)
            dprojected[rows, 2 * channels + at : 2 * channels + at + half] = dot(
                chances_held[n], dctx_held[n], 1, 0
            ).astype(BF16)

    for b in range(3):
        grads[channels * b : channels * (b + 1), :] = dot(
            shifted[...], dprojected[:, channels * b : channels * (b + 1)], 0, 0
        ).astype(BF16)
    grads[3 * channels : 4 * channels, :] = dot(context[...], dattended[...], 0, 0).astype(BF16)
    mine = lax.axis_index("col")
    keep[...] = grads[pl.ds(pl.multiple_of(mine * 2 * channels, 2 * channels), 2 * channels), :]
    send[...] = grads[
        pl.ds(pl.multiple_of((1 - mine) * 2 * channels, 2 * channels), 2 * channels), :
    ]

    full = dot(context[...], wproj[...], 1, 0)
    for w in range(windows):
        tile = full[cells * w : cells * (w + 1)].reshape(WIN, WIN, channels).astype(BF16)
        att_keep[:, WIN * w : WIN * (w + 1), :] = tile[0:SHIFT]
        both_send[0, :, WIN * w : WIN * (w + 1), :] = tile[SHIFT:WIN]
    full = dot(dprojected[...], wqkv[...], 1, 1)
    for w in range(windows):
        tile = full[cells * w : cells * (w + 1)].reshape(WIN, WIN, channels).astype(BF16)
        dn_keep[:, WIN * w : WIN * (w + 1), :] = tile[0:SHIFT]
        both_send[1, :, WIN * w : WIN * (w + 1), :] = tile[SHIFT:WIN]


def finish_kernel(
    feat, cot, domain, gain, att_keep, dn_keep, both_rows, edges,
    updated, grad_features,
    buf,
):
    tile_rows, cols, channels = feat.shape
    masks = domain_rows(domain, range(WIN), channels)

    def unshifted(slot, stayed, came):
        buf[0:SHIFT, 0:WIN, :] = edges[2 * slot].astype(F32)
        buf[SHIFT:WIN, 0:WIN, :] = edges[2 * slot + 1].astype(F32)
        buf[0:SHIFT, WIN : WIN + cols, :] = came[...].astype(F32)
        buf[SHIFT:WIN, WIN : WIN + cols, :] = stayed[...].astype(F32)

    unshifted(0, att_keep, both_rows.at[0])
    for i in range(WIN):
        back = buf[i, SHIFT : SHIFT + cols, :]
        updated[i] = (feat[i].astype(F32) + masks[i] * back).astype(BF16)
    unshifted(1, dn_keep, both_rows.at[1])
    for i in range(WIN):
        upstream = buf[i, SHIFT : SHIFT + cols, :] * gain[...]
        x = feat[i].astype(F32)
        centred = x - jnp.mean(x, -1, keepdims=True)
        variance = jnp.mean(centred * centred, -1, keepdims=True)
        inverse = lax.rsqrt(variance + NORM_EPSILON)
        standard = centred * inverse
        along = jnp.mean(upstream * standard, -1, keepdims=True)
        flat = jnp.mean(upstream, -1, keepdims=True)
        grad = inverse * (upstream - flat - standard * along)
        grad_features[i] = (cot[i].astype(F32) + grad).astype(BF16)


def sums_kernel(half, col_peer, wqkv, gain, grad_qkv, grad_proj, grad_gain, halves):
    channels = wqkv.shape[0]
    mine = lax.axis_index("col")
    halves[mine] = half[...].astype(F32)
    halves[1 - mine] = col_peer[...].astype(F32)
    total = jnp.zeros((8, channels), F32)
    ones = jnp.ones((8, channels), BF16)
    for b in range(3):
        part = halves[b // 2, channels * (b % 2) : channels * (b % 2 + 1), :]
        grad_qkv[:, channels * b : channels * (b + 1)] = part
        product = part * wqkv[:, channels * b : channels * (b + 1)].astype(F32)
        high = product.astype(BF16)
        low = (product - high.astype(F32)).astype(BF16)
        total = total + dot(ones, high, 1, 1) + dot(ones, low, 1, 1)
    grad_proj[...] = halves[1, channels:, :]
    grad_gain[...] = total[0:1, :] / gain[...]


VMEM = pl.BlockSpec(memory_space=pltpu.MemorySpace.VMEM)
HBM = pl.BlockSpec(memory_space=pltpu.MemorySpace.HBM)


def run(kernel, out_shapes, scratch, *operands, unstaged=()):
    operands = [
        pltpu.with_memory_space_constraint(a, pltpu.MemorySpace.HBM) if i in unstaged else a
        for i, a in enumerate(operands)
    ]
    return pl.pallas_call(
        kernel,
        out_shape=out_shapes,
        in_specs=[HBM if i in unstaged else VMEM for i in range(len(operands))],
        scratch_shapes=scratch,
        compiler_params=pltpu.CompilerParams(vmem_limit_bytes=48 << 20),
    )(*operands)


def ahead(array, axes):
    sizes = [lax.axis_size(a) for a in axes]
    if len(axes) == 1:
        pairs = [(i, (i - 1) % sizes[0]) for i in range(sizes[0])]
    else:
        rows, cols = sizes
        pairs = [
            (r * cols + c, (r - 1) % rows * cols + (c - 1) % cols)
            for r in range(rows)
            for c in range(cols)
        ]
    return lax.ppermute(array, axes if len(axes) > 1 else axes[0], pairs)


def behind(array, axis):
    peers = lax.axis_size(axis)
    return lax.ppermute(array, axis, [(i, (i + 1) % peers) for i in range(peers)])


def swap(array, axis, bit):
    return lax.ppermute(array, axis, [(i, i ^ bit) for i in range(lax.axis_size(axis))])


def add16(left, right):
    return (left.astype(F32) + right.astype(F32)).astype(BF16)


def on_device(features, cotangent, domain, qkv_weight, proj_weight, norm_gain):
    tile_rows, cols, channels = features.shape
    gain = norm_gain.reshape(1, channels)
    tokens = tile_rows * cols

    def shape(dims, dtype):
        return jax.ShapeDtypeStruct(dims, dtype)

    rows_out, right_out, corner_out, cotangent, domain = run(
        pack_kernel,
        (
            shape((2, SHIFT, cols, channels), BF16),
            shape((2, SHIFT, WIN, channels), BF16),
            shape((2, SHIFT, WIN, channels), BF16),
            shape(cotangent.shape, cotangent.dtype),
            shape(domain.shape, domain.dtype),
        ),
        [pltpu.SemaphoreType.DMA((5,))],
        features, cotangent, domain,
        unstaged=(0, 1, 2),
    )
    qkv_weight, proj_weight, gain, right_out = lax.optimization_barrier(
        (qkv_weight, proj_weight, gain, right_out)
    )
    qkv_weight, proj_weight, gain = run(
        fetch_kernel,
        (
            shape(qkv_weight.shape, qkv_weight.dtype),
            shape(proj_weight.shape, proj_weight.dtype),
            shape(gain.shape, gain.dtype),
        ),
        [pltpu.SemaphoreType.DMA((3,))],
        qkv_weight, proj_weight, gain,
        unstaged=(0, 1, 2),
    )
    below = ahead(rows_out, ("row",))
    right = ahead(right_out, ("col",))
    corner = ahead(corner_out, ("row", "col"))

    strip = shape((SHIFT, cols, channels), BF16)
    keep, send, att_keep, dn_keep, both_send = run(
        block_kernel,
        (
            shape((2 * channels, channels), BF16),
            shape((2 * channels, channels), BF16),
            strip,
            strip,
            shape((2, SHIFT, cols, channels), BF16),
        ),
        [
            pltpu.VMEM((WIN, cols + WIN, channels), F32),
            pltpu.VMEM((tokens, channels), BF16),
            pltpu.VMEM((tokens, 3 * channels), BF16),
            pltpu.VMEM((tokens, channels), BF16),
            pltpu.VMEM((tokens, channels), BF16),
            pltpu.VMEM((tokens, channels), BF16),
            pltpu.VMEM((tokens, 3 * channels), BF16),
            pltpu.VMEM((4 * channels, channels), BF16),
            pltpu.VMEM((8, 4 * WIN * WIN, channels // 2), BF16),
            pltpu.VMEM((8, 4 * WIN * WIN, channels // 2), BF16),
            pltpu.VMEM((8, WIN * WIN, 4 * WIN * WIN), F32),
            pltpu.VMEM((8, WIN * WIN, 4 * WIN * WIN), F32),
            pltpu.VMEM((8, WIN * WIN, 4 * WIN * WIN), BF16),
            pltpu.VMEM((8, WIN * WIN, 4 * WIN * WIN), BF16),
        ],
        features, cotangent, domain, below, right, corner, qkv_weight, proj_weight, gain,
    )
    summed = add16(keep, swap(send, "col", 1))
    place = lax.axis_index("row") % 4
    chunk = channels // 2

    def piece(step):
        return lax.dynamic_slice_in_dim(summed, (place ^ step) * chunk, chunk, 0)

    both_rows = behind(both_send, "row")
    received = [swap(piece(step), "row", step) for step in (1, 2, 3)]
    own = piece(0).astype(F32)
    for part in received:
        own = own + part.astype(F32)
    own = own.astype(BF16)
    own, both_rows = lax.optimization_barrier((own, both_rows))
    bit = 4
    while bit < lax.axis_size("row"):
        received = swap(own, "row", bit)
        own = add16(own, received)
        bit *= 2
    edges = jnp.stack(
        [part[:, cols - WIN :] for part in (both_rows[0], att_keep, both_rows[1], dn_keep)], 0
    )
    edges = behind(edges, "col")
    half = jnp.zeros((2 * channels, channels), BF16)
    parts = [own] + [swap(own, "row", step) for step in (1, 2, 3)]
    for step, part in enumerate(parts):
        half = lax.dynamic_update_slice_in_dim(half, part, (place ^ step) * chunk, 0)
    updated, grad_features = run(
        finish_kernel,
        (shape(features.shape, BF16), shape(features.shape, BF16)),
        [pltpu.VMEM((WIN, cols + WIN, channels), F32)],
        features, cotangent, domain, gain, att_keep, dn_keep, both_rows, edges,
    )
    half, updated, grad_features = lax.optimization_barrier((half, updated, grad_features))
    col_peer = swap(half, "col", 1)
    grad_qkv, grad_proj, grad_gain = run(
        sums_kernel,
        (
            shape((channels, 3 * channels), F32),
            shape((channels, channels), F32),
            shape((1, channels), F32),
        ),
        [pltpu.VMEM((2, 2 * channels, channels), F32)],
        half, col_peer, qkv_weight, gain,
    )
    return updated, grad_features, grad_qkv, grad_proj, grad_gain.reshape(channels)


def solution(mesh):
    return jax.shard_map(
        on_device,
        mesh=mesh,
        in_specs=(
            P(("grp", "row"), "col", None),
            P(("grp", "row"), "col", None),
            P(("grp", "row"), "col"),
            P(),
            P(),
            P(),
        ),
        out_specs=(
            P(("grp", "row"), "col", None),
            P(("grp", "row"), "col", None),
            P("grp", None),
            P("grp", None),
            P("grp"),
        ),
        check_vma=False,
    )
```

```python
import jax
import jax.numpy as jnp
from jax import lax
from jax.experimental import pallas as pl
from jax.experimental.pallas import tpu as pltpu
from jax.sharding import PartitionSpec as P

HEADS = 8
WIN = 8
SHIFT = 4
NORM_EPSILON = 1e-05
MASKED_SCORE = -1e30
LOG2_E = 1.4426950408889634

BF16 = jnp.bfloat16
F32 = jnp.float32


def dot(left, right, left_dim, right_dim):
    return lax.dot_general(
        left, right, (((left_dim,), (right_dim,)), ((), ())), preferred_element_type=F32
    )


def assemble_shifted(buf, own, below, right, corner):
    cols = own.shape[1]
    buf[0:SHIFT, 0:cols, :] = own
    buf[SHIFT:WIN, 0:cols, :] = below[...].astype(F32)
    buf[0:SHIFT, cols : cols + WIN, :] = right[...].astype(F32)
    buf[SHIFT:WIN, cols : cols + WIN, :] = corner[...].astype(F32)


def domain_rows(domain, rows, channels):
    flags = domain[...].astype(F32).astype(BF16)
    row_ids = lax.broadcasted_iota(jnp.int32, (flags.shape[0], channels), 0)
    return [dot(flags, (row_ids == row).astype(F32).astype(BF16), 0, 0) for row in rows]


def pack_kernel(
    feat, cot, domain_hbm,
    rows_out, right_out, corner_out, held, domain,
    sems,
):
    channels = feat.shape[-1]
    copies = [
        pltpu.make_async_copy(source, target, sems.at[i])
        for i, (source, target) in enumerate((
            (domain_hbm, domain),
            (cot, held),
            (feat.at[0:SHIFT], rows_out.at[0]),
            (feat.at[SHIFT:WIN, 0:WIN], right_out.at[0]),
            (feat.at[0:SHIFT, 0:WIN], corner_out.at[0]),
        ))
    ]
    for copy in copies:
        copy.start()
    copies[0].wait()
    masks = domain_rows(domain, range(WIN), channels)
    copies[1].wait()
    for i in range(SHIFT):
        masked = held[i].astype(F32) * masks[i]
        rows_out[1, i] = masked.astype(BF16)
        corner_out[1, i] = masked[0:WIN].astype(BF16)
        edge = held[SHIFT + i, 0:WIN, :].astype(F32) * masks[SHIFT + i][0:WIN]
        right_out[1, i] = edge.astype(BF16)
    for copy in copies[2:]:
        copy.wait()


def fetch_kernel(wqkv_hbm, wproj_hbm, gain_hbm, wqkv, wproj, gain, sems):
    pairs = ((wqkv_hbm, wqkv), (wproj_hbm, wproj), (gain_hbm, gain))
    copies = [pltpu.make_async_copy(a, b, sems.at[i]) for i, (a, b) in enumerate(pairs)]
    for copy in copies:
        copy.start()
    for copy in copies:
        copy.wait()


def block_kernel(
    feat, cot, domain, below, right, corner, wqkv, wproj, gain,
    keep, send, context, dprojected,
    buf, shifted, projected, dattended, dcontext, grads,
    query_held, dctx_held, scores_held, dchances_held, chances_held, dscore_held,
):
    tile_rows, cols, channels = feat.shape
    windows = cols // WIN
    cells = WIN * WIN
    half = channels // 2
    group_heads = HEADS // 2
    head_dim = channels // HEADS

    assemble_shifted(buf, feat[SHIFT:WIN].astype(F32), below.at[0], right.at[0], corner.at[0])
    x = buf[:, SHIFT : SHIFT + cols, :]
    centred = x - jnp.mean(x, -1, keepdims=True)
    variance = jnp.mean(centred * centred, -1, keepdims=True)
    normed = centred * lax.rsqrt(variance + NORM_EPSILON) * gain[...].reshape(1, 1, channels)
    for w in range(windows):
        tile = normed[:, WIN * w : WIN * (w + 1), :].reshape(cells, channels)
        shifted[cells * w : cells * (w + 1), :] = tile.astype(BF16)

    masks = domain_rows(domain, range(SHIFT, WIN), channels)
    own = jnp.stack([cot[SHIFT + i].astype(F32) * masks[i] for i in range(SHIFT)], 0)
    assemble_shifted(buf, own, below.at[1], right.at[1], corner.at[1])
    for w in range(windows):
        x = buf[:, SHIFT + WIN * w : SHIFT + WIN * (w + 1), :].reshape(cells, channels)
        dattended[cells * w : cells * (w + 1), :] = x.astype(BF16)

    projected[...] = dot(shifted[...], wqkv[...], 1, 0).astype(BF16)
    dcontext[...] = dot(dattended[...], wproj[...], 1, 1).astype(BF16)

    last_row = lax.axis_index("row") == lax.axis_size("row") - 1
    last_col = lax.axis_index("col") == lax.axis_size("col") - 1
    wide = group_heads * cells
    key_id = lax.broadcasted_iota(jnp.int32, (cells, wide), 0)
    query_id = lax.broadcasted_iota(jnp.int32, (cells, wide), 1)
    row_apart = ((key_id ^ query_id) & (WIN * SHIFT)) != 0
    col_apart = ((key_id ^ query_id) & SHIFT) != 0
    lane = lax.broadcasted_iota(jnp.int32, (cells, half), 1)
    in_head = [lane // head_dim == h for h in range(group_heads)]
    scale = head_dim ** (-0.5)

    def spread(values):
        zero = jnp.zeros_like(values)
        return jnp.concatenate([jnp.where(m, values, zero) for m in in_head], 0)

    def gather(full):
        parts = [full[cells * h : cells * (h + 1)] for h in range(group_heads)]
        out = parts[-1]
        for h in range(group_heads - 2, -1, -1):
            out = jnp.where(in_head[h], parts[h], out)
        return out

    row_excluded = jnp.logical_and(row_apart, last_row)
    groups = [(w, g) for w in range(windows) for g in range(2)]
    depth = scores_held.shape[0]
    for first in range(0, len(groups), depth):
        batch = groups[first : first + depth]
        for n, (w, g) in enumerate(batch):
            rows = slice(cells * w, cells * (w + 1))
            at = half * g
            query_x = spread(projected[rows, at : at + half])
            key = projected[rows, channels + at : channels + at + half]
            value = projected[rows, 2 * channels + at : 2 * channels + at + half]
            dctx_x = spread(dcontext[rows, at : at + half])
            query_held[n] = query_x
            dctx_held[n] = dctx_x
            scores_held[n] = dot(key, query_x, 1, 1)
            dchances_held[n] = dot(value, dctx_x, 1, 1)
        for n, (w, g) in enumerate(batch):
            excluded = row_excluded
            if w == windows - 1:
                excluded = jnp.logical_or(excluded, jnp.logical_and(col_apart, last_col))
            scores = jnp.where(excluded, MASKED_SCORE, scores_held[n])
            peak = jnp.max(scores, 0, keepdims=True)
            weights = jnp.exp2((scores - peak) * (scale * LOG2_E))
            chances = weights * (1.0 / jnp.sum(weights, 0, keepdims=True))
            chances_held[n] = chances.astype(BF16)
            dchances = dchances_held[n].astype(BF16).astype(F32)
            mean = jnp.sum(chances * dchances, 0, keepdims=True)
            dscore_held[n] = (chances * (dchances - mean) * scale).astype(BF16)
        for n, (w, g) in enumerate(batch):
            rows = slice(cells * w, cells * (w + 1))
            at = half * g
            key = projected[rows, channels + at : channels + at + half]
            value = projected[rows, 2 * channels + at : 2 * channels + at + half]
            context[rows, at : at + half] = gather(dot(chances_held[n], value, 0, 0)).astype(BF16)
            dprojected[rows, at : at + half] = gather(dot(dscore_held[n], key, 0, 0)).astype(BF16)
            dprojected[rows, channels + at : channels + at + half] = dot(
                dscore_held[n], query_held[n], 1, 0
            ).astype(BF16)
            dprojected[rows, 2 * channels + at : 2 * channels + at + half] = dot(
                chances_held[n], dctx_held[n], 1, 0
            ).astype(BF16)

    for b in range(3):
        grads[channels * b : channels * (b + 1), :] = dot(
            shifted[...], dprojected[:, channels * b : channels * (b + 1)], 0, 0
        ).astype(BF16)
    grads[3 * channels : 4 * channels, :] = dot(context[...], dattended[...], 0, 0).astype(BF16)
    mine = lax.axis_index("col")
    keep[...] = grads[pl.ds(pl.multiple_of(mine * 2 * channels, 2 * channels), 2 * channels), :]
    send[...] = grads[
        pl.ds(pl.multiple_of((1 - mine) * 2 * channels, 2 * channels), 2 * channels), :
    ]


def results_kernel(context, dprojected, wproj, wqkv, att_keep, dn_keep, both_send):
    channels = wproj.shape[0]
    cells = WIN * WIN
    windows = context.shape[0] // cells
    full = dot(context[...], wproj[...], 1, 0)
    for w in range(windows):
        tile = full[cells * w : cells * (w + 1)].reshape(WIN, WIN, channels).astype(BF16)
        att_keep[:, WIN * w : WIN * (w + 1), :] = tile[0:SHIFT]
        both_send[0, :, WIN * w : WIN * (w + 1), :] = tile[SHIFT:WIN]
    full = dot(dprojected[...], wqkv[...], 1, 1)
    for w in range(windows):
        tile = full[cells * w : cells * (w + 1)].reshape(WIN, WIN, channels).astype(BF16)
        dn_keep[:, WIN * w : WIN * (w + 1), :] = tile[0:SHIFT]
        both_send[1, :, WIN * w : WIN * (w + 1), :] = tile[SHIFT:WIN]


def finish_kernel(
    feat, cot, domain, gain, att_keep, dn_keep, both_rows, edges,
    updated, grad_features,
    buf,
):
    tile_rows, cols, channels = feat.shape
    masks = domain_rows(domain, range(WIN), channels)

    def unshifted(slot, stayed, came):
        buf[0:SHIFT, 0:WIN, :] = edges[2 * slot].astype(F32)
        buf[SHIFT:WIN, 0:WIN, :] = edges[2 * slot + 1].astype(F32)
        buf[0:SHIFT, WIN : WIN + cols, :] = came[...].astype(F32)
        buf[SHIFT:WIN, WIN : WIN + cols, :] = stayed[...].astype(F32)

    unshifted(0, att_keep, both_rows.at[0])
    for i in range(WIN):
        back = buf[i, SHIFT : SHIFT + cols, :]
        updated[i] = (feat[i].astype(F32) + masks[i] * back).astype(BF16)
    unshifted(1, dn_keep, both_rows.at[1])
    for i in range(WIN):
        upstream = buf[i, SHIFT : SHIFT + cols, :] * gain[...]
        x = feat[i].astype(F32)
        centred = x - jnp.mean(x, -1, keepdims=True)
        variance = jnp.mean(centred * centred, -1, keepdims=True)
        inverse = lax.rsqrt(variance + NORM_EPSILON)
        standard = centred * inverse
        along = jnp.mean(upstream * standard, -1, keepdims=True)
        flat = jnp.mean(upstream, -1, keepdims=True)
        grad = inverse * (upstream - flat - standard * along)
        grad_features[i] = (cot[i].astype(F32) + grad).astype(BF16)


def sums_kernel(half, col_peer, wqkv, gain, grad_qkv, grad_proj, grad_gain, halves):
    channels = wqkv.shape[0]
    mine = lax.axis_index("col")
    halves[mine] = half[...].astype(F32)
    halves[1 - mine] = col_peer[...].astype(F32)
    total = jnp.zeros((8, channels), F32)
    ones = jnp.ones((8, channels), BF16)
    for b in range(3):
        part = halves[b // 2, channels * (b % 2) : channels * (b % 2 + 1), :]
        grad_qkv[:, channels * b : channels * (b + 1)] = part
        product = part * wqkv[:, channels * b : channels * (b + 1)].astype(F32)
        high = product.astype(BF16)
        low = (product - high.astype(F32)).astype(BF16)
        total = total + dot(ones, high, 1, 1) + dot(ones, low, 1, 1)
    grad_proj[...] = halves[1, channels:, :]
    grad_gain[...] = total[0:1, :] / gain[...]


VMEM = pl.BlockSpec(memory_space=pltpu.MemorySpace.VMEM)
HBM = pl.BlockSpec(memory_space=pltpu.MemorySpace.HBM)


def run(kernel, out_shapes, scratch, *operands, unstaged=()):
    operands = [
        pltpu.with_memory_space_constraint(a, pltpu.MemorySpace.HBM) if i in unstaged else a
        for i, a in enumerate(operands)
    ]
    return pl.pallas_call(
        kernel,
        out_shape=out_shapes,
        in_specs=[HBM if i in unstaged else VMEM for i in range(len(operands))],
        scratch_shapes=scratch,
        compiler_params=pltpu.CompilerParams(vmem_limit_bytes=48 << 20),
    )(*operands)


def ahead(array, axes):
    sizes = [lax.axis_size(a) for a in axes]
    if len(axes) == 1:
        pairs = [(i, (i - 1) % sizes[0]) for i in range(sizes[0])]
    else:
        rows, cols = sizes
        pairs = [
            (r * cols + c, (r - 1) % rows * cols + (c - 1) % cols)
            for r in range(rows)
            for c in range(cols)
        ]
    return lax.ppermute(array, axes if len(axes) > 1 else axes[0], pairs)


def behind(array, axis):
    peers = lax.axis_size(axis)
    return lax.ppermute(array, axis, [(i, (i + 1) % peers) for i in range(peers)])


def swap(array, axis, bit):
    return lax.ppermute(array, axis, [(i, i ^ bit) for i in range(lax.axis_size(axis))])


def add16(left, right):
    return (left.astype(F32) + right.astype(F32)).astype(BF16)


def on_device(features, cotangent, domain, qkv_weight, proj_weight, norm_gain):
    tile_rows, cols, channels = features.shape
    gain = norm_gain.reshape(1, channels)
    tokens = tile_rows * cols

    def shape(dims, dtype):
        return jax.ShapeDtypeStruct(dims, dtype)

    rows_out, right_out, corner_out, cotangent, domain = run(
        pack_kernel,
        (
            shape((2, SHIFT, cols, channels), BF16),
            shape((2, SHIFT, WIN, channels), BF16),
            shape((2, SHIFT, WIN, channels), BF16),
            shape(cotangent.shape, cotangent.dtype),
            shape(domain.shape, domain.dtype),
        ),
        [pltpu.SemaphoreType.DMA((5,))],
        features, cotangent, domain,
        unstaged=(0, 1, 2),
    )
    qkv_weight, proj_weight, gain, right_out = lax.optimization_barrier(
        (qkv_weight, proj_weight, gain, right_out)
    )
    qkv_weight, proj_weight, gain = run(
        fetch_kernel,
        (
            shape(qkv_weight.shape, qkv_weight.dtype),
            shape(proj_weight.shape, proj_weight.dtype),
            shape(gain.shape, gain.dtype),
        ),
        [pltpu.SemaphoreType.DMA((3,))],
        qkv_weight, proj_weight, gain,
        unstaged=(0, 1, 2),
    )
    below = ahead(rows_out, ("row",))
    right = ahead(right_out, ("col",))
    corner = ahead(corner_out, ("row", "col"))

    strip = shape((SHIFT, cols, channels), BF16)
    keep, send, context, dprojected = run(
        block_kernel,
        (
            shape((2 * channels, channels), BF16),
            shape((2 * channels, channels), BF16),
            shape((tokens, channels), BF16),
            shape((tokens, 3 * channels), BF16),
        ),
        [
            pltpu.VMEM((WIN, cols + WIN, channels), F32),
            pltpu.VMEM((tokens, channels), BF16),
            pltpu.VMEM((tokens, 3 * channels), BF16),
            pltpu.VMEM((tokens, channels), BF16),
            pltpu.VMEM((tokens, channels), BF16),
            pltpu.VMEM((4 * channels, channels), BF16),
            pltpu.VMEM((8, 4 * WIN * WIN, channels // 2), BF16),
            pltpu.VMEM((8, 4 * WIN * WIN, channels // 2), BF16),
            pltpu.VMEM((8, WIN * WIN, 4 * WIN * WIN), F32),
            pltpu.VMEM((8, WIN * WIN, 4 * WIN * WIN), F32),
            pltpu.VMEM((8, WIN * WIN, 4 * WIN * WIN), BF16),
            pltpu.VMEM((8, WIN * WIN, 4 * WIN * WIN), BF16),
        ],
        features, cotangent, domain, below, right, corner, qkv_weight, proj_weight, gain,
    )
    strip = shape((SHIFT, cols, channels), BF16)
    att_keep, dn_keep, both_send = run(
        results_kernel,
        (strip, strip, shape((2, SHIFT, cols, channels), BF16)),
        [],
        context, dprojected, proj_weight, qkv_weight,
    )

    summed = add16(keep, swap(send, "col", 1))
    place = lax.axis_index("row") % 4
    chunk = channels // 2

    def piece(step):
        return lax.dynamic_slice_in_dim(summed, (place ^ step) * chunk, chunk, 0)

    both_rows = behind(both_send, "row")
    received = [swap(piece(step), "row", step) for step in (1, 2, 3)]
    own = piece(0).astype(F32)
    for part in received:
        own = own + part.astype(F32)
    own = own.astype(BF16)
    bit = 4
    while bit < lax.axis_size("row"):
        received = swap(own, "row", bit)
        own = add16(own, received)
        bit *= 2
    own, both_rows = lax.optimization_barrier((own, both_rows))
    edges = jnp.stack(
        [part[:, cols - WIN :] for part in (both_rows[0], att_keep, both_rows[1], dn_keep)], 0
    )
    edges = behind(edges, "col")
    half = jnp.zeros((2 * channels, channels), BF16)
    parts = [own] + [swap(own, "row", step) for step in (1, 2, 3)]
    for step, part in enumerate(parts):
        half = lax.dynamic_update_slice_in_dim(half, part, (place ^ step) * chunk, 0)
    updated, grad_features = run(
        finish_kernel,
        (shape(features.shape, BF16), shape(features.shape, BF16)),
        [pltpu.VMEM((WIN, cols + WIN, channels), F32)],
        features, cotangent, domain, gain, att_keep, dn_keep, both_rows, edges,
    )
    half, updated, grad_features = lax.optimization_barrier((half, updated, grad_features))
    col_peer = swap(half, "col", 1)
    grad_qkv, grad_proj, grad_gain = run(
        sums_kernel,
        (
            shape((channels, 3 * channels), F32),
            shape((channels, channels), F32),
            shape((1, channels), F32),
        ),
        [pltpu.VMEM((2, 2 * channels, channels), F32)],
        half, col_peer, qkv_weight, gain,
    )
    return updated, grad_features, grad_qkv, grad_proj, grad_gain.reshape(channels)


def solution(mesh):
    return jax.shard_map(
        on_device,
        mesh=mesh,
        in_specs=(
            P(("grp", "row"), "col", None),
            P(("grp", "row"), "col", None),
            P(("grp", "row"), "col"),
            P(),
            P(),
            P(),
        ),
        out_specs=(
            P(("grp", "row"), "col", None),
            P(("grp", "row"), "col", None),
            P("grp", None),
            P("grp", None),
            P("grp"),
        ),
        check_vma=False,
    )
```
